32 devices in a mesh: dp: 32 (over z, y, x, core).
Axes of the slice: x: 2, y: 2, z: 4, core: 2. Of those that a mesh axis runs over, the one named last changes fastest.
Arguments:
- tokens: bfloat16 [32768, 512], P('dp'), may hold values from -6 to 6
- timesteps: int32 [32], P('dp'), may hold values from 0 to 49
- w_qkv: bfloat16 [512, 1536], P('dp'), may hold values from -0.375 to 0.375
- w_out: bfloat16 [512, 512], P('dp'), may hold values from -1 to 1
- w_up: bfloat16 [512, 2048], P('dp'), may hold values from -0.25 to 0.25
- w_down: bfloat16 [2048, 512], P('dp'), may hold values from -0.1875 to 0.1875
- gain_attn: bfloat16 [512], P('dp'), may hold values from 0.25 to 1.75
- shift_attn: bfloat16 [512], P('dp'), may hold values from -1.75 to 1.75
- gain_ffn: bfloat16 [512], P('dp'), may hold values from 0.25 to 1.75
- shift_ffn: bfloat16 [512], P('dp'), may hold values from -1.75 to 1.75
- bias_query: bfloat16 [512], P('dp'), may hold values from -3 to 3
- bias_value: bfloat16 [512], P('dp'), may hold values from -3 to 3
- bias_out: bfloat16 [512], P('dp'), may hold values from -3 to 3
- bias_up: bfloat16 [2048], P('dp'), may hold values from -3 to 3
- bias_down: bfloat16 [512], P('dp'), may hold values from -3 to 3
- step_table: bfloat16 [50, 512], P(None, 'dp'), may hold values from -3 to 3
- cotangent: bfloat16 [32768, 512], P('dp'), may hold values from -6 to 6
Outputs:
- output: bfloat16 [32768, 512], P('dp')
- grad_tokens: float32 [32768, 512], P('dp')
- grad_w_qkv: float32 [512, 1536], P('dp')
- grad_w_out: float32 [512, 512], P('dp')
- grad_w_up: float32 [512, 2048], P('dp')
- grad_w_down: float32 [2048, 512], P('dp')
- grad_gain_attn: float32 [512], P('dp')
- grad_shift_attn: float32 [512], P('dp')
- grad_gain_ffn: float32 [512], P('dp')
- grad_shift_ffn: float32 [512], P('dp')
- grad_bias_query: float32 [512], P('dp')
- grad_bias_value: float32 [512], P('dp')
- grad_bias_out: float32 [512], P('dp')
- grad_bias_up: float32 [2048], P('dp')
- grad_bias_down: float32 [512], P('dp')
- grad_step_table: float32 [50, 512], P(None, 'dp')
The draws below stay inside these ranges and needn't reach their ends.
All inputs are finite; a program needn't handle non-finite values.
Results may differ from the reference program's by a relative error of at most 0.014.
Values may be sent and summed in bfloat16 or wider, within the bound.
No kernel may reach another device: no remote copies, remote signals or barrier semaphores. Data moves between devices by JAX's collectives and lax.ppermute only.
A program may use at most 192 MiB of HBM per device.

```python
import jax
import jax.numpy as jnp
from jax import lax

D = 512
HEADS = 8
HEAD_DIM = 64
FF = 2048
TSTEPS = 50
SEG_LEN = 1024
SEGS = 32
TOKENS = 32768


def plant(values, own_key, least, top_value):
    spot = [jax.random.randint(jax.random.fold_in(own_key, axis), (), 0, length) for axis, length in enumerate(values.shape)]
    longest = values.shape.index(max(values.shape))
    next_to = spot[:longest] + [(spot[longest] + 1) % values.shape[longest]] + spot[longest + 1:]
    return values.at[tuple(spot)].set(least).at[tuple(next_to)].set(top_value)


def shard_levels(key, dims, pieces, least, largest):
    def one(axis_at, shards_of):
        steps = jax.random.uniform(jax.random.fold_in(jax.random.fold_in(key, 6), axis_at), (shards_of,), jnp.float32, least / len(pieces), largest / len(pieces))
        return jnp.repeat(jnp.exp(steps), dims[axis_at] // shards_of).reshape((-1,) + (1,) * (len(dims) - axis_at - 1))

    level = one(*pieces[0])
    for cut in pieces[1:]:
        level = level * one(*cut)
    return level


def gaussian(rng, dims, deviation, bound, cuts=(), dtype=jnp.bfloat16):
    factor_of = shard_levels(rng, dims, cuts, -0.22, 0.18) if cuts else 1.0
    drawn = jax.random.normal(rng, dims, jnp.float32) * deviation * factor_of
    return jnp.minimum(jnp.maximum(drawn, -bound), bound).astype(dtype)


def setup_inputs(seed: int = 0) -> dict:
    arg_keys = jax.random.split(jax.random.key(seed), 18)
    return {
        "tokens": gaussian(arg_keys[0], (TOKENS, D), 1.0, 6.0, ((0, 32),)),
        "timesteps": plant(jax.random.randint(arg_keys[1], (SEGS,), 0, TSTEPS), jax.random.fold_in(arg_keys[1], 1), 0, TSTEPS - 1).astype(jnp.int32),
        "w_qkv": gaussian(arg_keys[2], (D, 3 * D), (D // 2) ** -0.5, 0.375, ((0, 32),)),
        "w_out": gaussian(arg_keys[3], (D, D), (D // 16) ** -0.5, 1.0, ((0, 32),)),
        "w_up": gaussian(arg_keys[4], (D, FF), D ** -0.5, 0.25, ((0, 32),)),
        "w_down": gaussian(arg_keys[5], (FF, D), (FF // 2) ** -0.5, 0.1875, ((0, 32),)),
        "gain_attn": jnp.clip(1.0 + 0.15 * jax.random.normal(arg_keys[6], (D,), jnp.float32), 0.25, 1.75).astype(jnp.bfloat16),
        "shift_attn": gaussian(arg_keys[7], (D,), 0.3, 1.75, ((0, 32),)),
        "gain_ffn": jnp.clip(1.0 + 0.15 * jax.random.normal(arg_keys[8], (D,), jnp.float32), 0.25, 1.75).astype(jnp.bfloat16),
        "shift_ffn": gaussian(arg_keys[9], (D,), 0.3, 1.75, ((0, 32),)),
        "bias_query": gaussian(arg_keys[10], (D,), 0.5, 3.0, ((0, 32),)),
        "bias_value": gaussian(arg_keys[11], (D,), 0.5, 3.0, ((0, 32),)),
        "bias_out": gaussian(arg_keys[12], (D,), 0.5, 3.0, ((0, 32),)),
        "bias_up": gaussian(arg_keys[13], (FF,), 0.5, 3.0, ((0, 32),)),
        "bias_down": gaussian(arg_keys[14], (D,), 0.5, 3.0, ((0, 32),)),
        "step_table": gaussian(arg_keys[15], (TSTEPS, D), 0.5, 3.0, ((1, 32),)),
        "cotangent": gaussian(arg_keys[16], (TOKENS, D), 1.0, 6.0, ((0, 32),)),
    }


@jax.custom_vjp
def low(v):
    return lax.optimization_barrier(v.astype(jnp.bfloat16)).astype(jnp.float32)

@jax.custom_vjp
def low_back(v):
    return v

def low_keep(v):
    return (low(v), None)

def low_pass(kept, grad):
    return (grad,)

def back_keep(v):
    return (v, None)

def back_low(kept, grad):
    return (low(grad),)
low.defvjp(low_keep, low_pass)
low_back.defvjp(back_keep, back_low)
EPSILON = 1e-05
HIGHEST = lax.Precision.HIGHEST

def layer_norm(hidden, gain, shift):
    centred = hidden - lax.optimization_barrier(jnp.mean(hidden, axis=-1, keepdims=True))
    variance = lax.optimization_barrier(jnp.mean(centred * centred, axis=-1, keepdims=True))
    return centred * lax.rsqrt(variance + EPSILON) * gain + shift

def matmul(left, right):
    return jnp.dot(left, right, precision=HIGHEST)

def segment_forward(params, seg_rows, step_row):
    w_qkv, w_out, w_up, w_down, gain_attn, shift_attn, gain_ffn, shift_ffn, bias_query, bias_value, bias_out, bias_up, bias_down, step_table = params
    start = seg_rows + step_row[None, :]
    attn_input = low(layer_norm(start, gain_attn, shift_attn))
    bias_cat = jnp.concatenate([bias_query, jnp.zeros_like(bias_query), bias_value])
    projected = low(low_back(matmul(attn_input, w_qkv) + bias_cat))
    seg_len = seg_rows.shape[0]
    heads_view = projected.reshape(seg_len, 3, HEADS, HEAD_DIM)
    queries = heads_view[:, 0]
    keys_in = heads_view[:, 1]
    values = heads_view[:, 2]
    scores = low_back(jnp.einsum('qhe,khe->hqk', queries, keys_in, precision=HIGHEST) * 0.125)
    probs = jax.nn.softmax(scores, axis=-1)
    mixed = jnp.einsum('hqk,khe->qhe', low(probs), values, precision=HIGHEST).reshape(seg_len, D)
    mixed = low(low_back(mixed))
    branch = low_back(matmul(mixed, w_out) + bias_out)
    middle = start + branch
    ffn_input = low(layer_norm(middle, gain_ffn, shift_ffn))
    pre_act = low_back(matmul(ffn_input, w_up) + bias_up)
    hidden_act = low(jax.nn.gelu(pre_act, approximate=False))
    feed_out = low_back(matmul(hidden_act, w_down) + bias_down)
    return middle + feed_out

def reference(tokens, timesteps, w_qkv, w_out, w_up, w_down, gain_attn, shift_attn, gain_ffn, shift_ffn, bias_query, bias_value, bias_out, bias_up, bias_down, step_table, cotangent):
    params = tuple((entry.astype(jnp.float32) for entry in (w_qkv, w_out, w_up, w_down, gain_attn, shift_attn, gain_ffn, shift_ffn, bias_query, bias_value, bias_out, bias_up, bias_down, step_table)))
    inputs = tokens.astype(jnp.float32)

    def forward(params, inputs):
        step_rows = jnp.take(params[13], timesteps, axis=0)
        seg_rows = inputs.reshape(SEGS, SEG_LEN, D)

        def one_segment(pair):
            return segment_forward(params, pair[0], pair[1])
        results = lax.map(jax.checkpoint(one_segment), (seg_rows, step_rows))
        return results.reshape(TOKENS, D)
    result, backward = jax.vjp(forward, params, inputs)
    grad_params, grad_inputs = backward(cotangent.astype(jnp.float32))
    return (result.astype(jnp.bfloat16), grad_inputs, grad_params[0], grad_params[1], grad_params[2], grad_params[3], grad_params[4], grad_params[5], grad_params[6], grad_params[7], grad_params[8], grad_params[9], grad_params[10], grad_params[11], grad_params[12], grad_params[13])
```

```python
import functools

import jax
import jax.numpy as jnp
from jax import lax
from jax.sharding import PartitionSpec as P

HEADS = 8
HEAD_DIM = 64


EPSILON = 1e-05
SCALE_FACTOR = 0.125


def normalize(hidden):
    centred = hidden - jnp.mean(hidden, axis=-1, keepdims=True)
    inverse = lax.rsqrt(jnp.mean(centred * centred, axis=-1, keepdims=True) + EPSILON)
    return (centred * inverse, inverse)


def norm_back(grad_out, gain, normed, inverse):
    scaled = grad_out * gain
    return inverse * (
        scaled
        - jnp.mean(scaled, axis=-1, keepdims=True)
        - normed * jnp.mean(scaled * normed, axis=-1, keepdims=True)
    )


def exact_gelu(value):
    return jax.nn.gelu(value, approximate=False)


def attend(operands):
    queries, keys_in, values = operands
    scores = (
        jnp.einsum("qhe,khe->hqk", queries, keys_in, preferred_element_type=jnp.float32)
        * SCALE_FACTOR
    )
    row_max = jnp.max(scores, axis=-1, keepdims=True)
    raised = jnp.exp(scores - row_max)
    row_sum = jnp.sum(raised, axis=-1, keepdims=True)
    weights = (raised / row_sum).astype(jnp.bfloat16)
    mixed_rows = jnp.einsum("hqk,khe->qhe", weights, values, preferred_element_type=jnp.float32)
    return (mixed_rows.astype(jnp.bfloat16), (row_max + jnp.log(row_sum))[..., 0])


def attend_back(operands):
    queries, keys_in, values, log_sum, grad_mix = operands
    scores = (
        jnp.einsum("qhe,khe->hqk", queries, keys_in, preferred_element_type=jnp.float32)
        * SCALE_FACTOR
    )
    probs = jnp.exp(scores - log_sum[..., None])
    grad_values = jnp.einsum(
        "hqk,qhe->khe", probs.astype(jnp.bfloat16), grad_mix, preferred_element_type=jnp.float32
    )
    grad_probs = jnp.einsum("qhe,khe->hqk", grad_mix, values, preferred_element_type=jnp.float32)
    grad_scores = (
        probs * (grad_probs - jnp.sum(probs * grad_probs, axis=-1, keepdims=True))
    ).astype(jnp.bfloat16)
    grad_queries = (
        jnp.einsum("hqk,khe->qhe", grad_scores, keys_in, preferred_element_type=jnp.float32)
        * SCALE_FACTOR
    )
    grad_keys = (
        jnp.einsum("hqk,qhe->khe", grad_scores, queries, preferred_element_type=jnp.float32)
        * SCALE_FACTOR
    )
    seg_len = queries.shape[0]
    joined = jnp.concatenate(
        [
            grad_queries.reshape(seg_len, -1),
            grad_keys.reshape(seg_len, -1),
            grad_values.reshape(seg_len, -1),
        ],
        axis=1,
    )
    return joined.astype(jnp.bfloat16)


def radices(count):
    sizes, rest = [2], count // 2
    while rest > 1:
        step = 4 if rest % 4 == 0 else (2 if rest % 2 == 0 else rest)
        sizes.append(step)
        rest //= step
    return sizes


def digit_groups(count, level):
    sizes = radices(count)
    stride = 1
    for size in sizes[:level]:
        stride *= size
    size = sizes[level]
    groups = []
    for base in range(count):
        if (base // stride) % size == 0:
            groups.append([base + stride * k for k in range(size)])
    return groups


def exchange(value, groups=None):
    return lax.all_to_all(value, "dp", 0, 0, tiled=True, axis_index_groups=groups)


def gather(shard, count):
    sizes = radices(count)
    value = shard
    for level in reversed(range(len(sizes))):
        spread = jnp.broadcast_to(value[None], (sizes[level],) + value.shape)
        value = exchange(spread, digit_groups(count, level))
    order = tuple(reversed(range(len(sizes))))
    value = value.transpose(order + tuple(range(len(sizes), value.ndim)))
    return value.reshape((count,) + shard.shape)


def scatter_sum(blocks):
    return jnp.sum(exchange(blocks).astype(jnp.float32), axis=0)


def per_device(
    count,
    tokens,
    timesteps,
    w_qkv,
    w_out,
    w_up,
    w_down,
    gain_attn,
    shift_attn,
    gain_ffn,
    shift_ffn,
    bias_query,
    bias_value,
    bias_out,
    bias_up,
    bias_down,
    step_table,
    cotangent,
):
    width = tokens.shape[1]
    own = width // count
    full_qkv = gather(w_qkv, count).reshape(width, -1)
    small = jnp.concatenate(
        [
            gain_attn,
            shift_attn,
            gain_ffn,
            shift_ffn,
            bias_query,
            bias_value,
            bias_out,
            bias_down,
            bias_up,
            step_table.reshape(-1),
            timesteps.astype(jnp.bfloat16),
        ]
    )
    small_all = exchange(jnp.broadcast_to(small[None], (count,) + small.shape))
    (
        attn_gain,
        attn_shift,
        feed_gain,
        feed_shift,
        query_bias,
        value_bias,
        out_bias,
        down_bias,
    ) = (small_all[:, k * own : (k + 1) * own].reshape(-1) for k in range(8))
    used = 8 * own
    hidden_own = bias_up.shape[0]
    up_bias = small_all[:, used : used + hidden_own].reshape(-1)
    used += hidden_own
    steps = step_table.shape[0]
    table_all = small_all[:, used : used + steps * own].reshape(count, steps, own)
    all_times = small_all[:, used + steps * own :].reshape(-1).astype(jnp.int32)
    full_table = table_all.transpose(1, 0, 2).reshape(steps, width)
    full_out = gather(w_out, count).reshape(width, -1)
    full_up = gather(w_up, count).reshape(width, -1)
    full_down = gather(w_down, count).reshape(-1, width)
    seg_count = timesteps.shape[0]
    seg_len = tokens.shape[0] // seg_count
    one_hot = timesteps[:, None] == jnp.arange(full_table.shape[0])[None, :]
    step_rows = jnp.dot(
        one_hot.astype(jnp.bfloat16), full_table, preferred_element_type=jnp.float32
    )
    start = (
        tokens.astype(jnp.float32).reshape(seg_count, seg_len, width) + step_rows[:, None, :]
    ).reshape(-1, width)
    attn_normed, attn_inverse = normalize(start)
    attn_input = (
        attn_normed * attn_gain.astype(jnp.float32) + attn_shift.astype(jnp.float32)
    ).astype(jnp.bfloat16)
    bias_cat = jnp.concatenate([query_bias, jnp.zeros_like(query_bias), value_bias]).astype(
        jnp.float32
    )
    projected = (
        jnp.dot(attn_input, full_qkv, preferred_element_type=jnp.float32) + bias_cat
    ).astype(jnp.bfloat16)
    heads_view = projected.reshape(seg_count, seg_len, 3, HEADS, HEAD_DIM)
    queries = heads_view[:, :, 0]
    keys_in = heads_view[:, :, 1]
    values = heads_view[:, :, 2]
    mixed, log_sums = lax.map(attend, (queries, keys_in, values))
    attn_rows = mixed.reshape(-1, width)
    middle = (
        start
        + jnp.dot(attn_rows, full_out, preferred_element_type=jnp.float32)
        + out_bias.astype(jnp.float32)
    )
    feed_normed, feed_inverse = normalize(middle)
    feed_input = (
        feed_normed * feed_gain.astype(jnp.float32) + feed_shift.astype(jnp.float32)
    ).astype(jnp.bfloat16)
    pre_act = jnp.dot(feed_input, full_up, preferred_element_type=jnp.float32) + up_bias.astype(
        jnp.float32
    )
    hidden_act = exact_gelu(pre_act).astype(jnp.bfloat16)
    result = (
        middle
        + jnp.dot(hidden_act, full_down, preferred_element_type=jnp.float32)
        + down_bias.astype(jnp.float32)
    )
    output = result.astype(jnp.bfloat16)
    grad_res = cotangent.astype(jnp.float32)
    grad_bdown = jnp.sum(grad_res, axis=0)
    grad_hidden = jnp.einsum("nd,fd->nf", cotangent, full_down, preferred_element_type=jnp.float32)
    gelu_value, gelu_back = jax.vjp(exact_gelu, pre_act)
    grad_pre = gelu_back(grad_hidden)[0].astype(jnp.bfloat16)
    grad_bup = jnp.sum(grad_pre.astype(jnp.float32), axis=0)
    grad_feed = jnp.einsum("nf,df->nd", grad_pre, full_up, preferred_element_type=jnp.float32)
    grad_gain_f = jnp.sum(grad_feed * feed_normed, axis=0)
    grad_shift_f = jnp.sum(grad_feed, axis=0)
    grad_mid = grad_res + norm_back(
        grad_feed, feed_gain.astype(jnp.float32), feed_normed, feed_inverse
    )
    grad_down = jnp.einsum("nf,nd->fd", hidden_act, cotangent, preferred_element_type=jnp.float32)
    grad_up = jnp.einsum("nd,nf->df", feed_input, grad_pre, preferred_element_type=jnp.float32)
    grad_branch = grad_mid.astype(jnp.bfloat16)
    grad_bout = jnp.sum(grad_branch.astype(jnp.float32), axis=0)
    grad_mixed = jnp.einsum(
        "ne,de->nd", grad_branch, full_out, preferred_element_type=jnp.float32
    ).astype(jnp.bfloat16)
    grad_proj = lax.map(
        attend_back,
        (
            queries,
            keys_in,
            values,
            log_sums,
            grad_mixed.reshape(seg_count, seg_len, HEADS, HEAD_DIM),
        ),
    )
    grad_proj = grad_proj.reshape(-1, 3 * width)
    proj_sums = jnp.sum(grad_proj.astype(jnp.float32), axis=0)
    grad_bquery = proj_sums[:width]
    grad_bvalue = proj_sums[2 * width :]
    grad_attn = jnp.einsum("ne,de->nd", grad_proj, full_qkv, preferred_element_type=jnp.float32)
    grad_gain_a = jnp.sum(grad_attn * attn_normed, axis=0)
    grad_shift_a = jnp.sum(grad_attn, axis=0)
    grad_start = grad_mid + norm_back(
        grad_attn, attn_gain.astype(jnp.float32), attn_normed, attn_inverse
    )
    seg_grads = jnp.sum(grad_start.reshape(seg_count, seg_len, width), axis=1)
    grad_wqkv = jnp.einsum("nd,ne->de", attn_input, grad_proj, preferred_element_type=jnp.float32)
    grad_wout = jnp.einsum("nd,ne->de", attn_rows, grad_branch, preferred_element_type=jnp.float32)
    sum_qkv, sum_out, sum_up, sum_down = (
        scatter_sum(grad.astype(jnp.bfloat16).reshape(count, -1, grad.shape[1]))
        for grad in (grad_wqkv, grad_wout, grad_up, grad_down)
    )
    early = scatter_sum(
        jnp.concatenate(
            [
                entry.reshape(count, -1)
                for entry in (grad_gain_f, grad_shift_f, grad_bout, grad_bdown, grad_bup)
            ],
            axis=1,
        )
    )
    late = exchange(
        jnp.concatenate(
            [
                entry.reshape(count, -1)
                for entry in (
                    grad_gain_a,
                    grad_shift_a,
                    grad_bquery,
                    grad_bvalue,
                    seg_grads.reshape(seg_count, count, own).transpose(1, 0, 2),
                )
            ],
            axis=1,
        )
    )
    late_sum = jnp.sum(late[:, : 4 * own], axis=0)
    segs = late[:, 4 * own :].reshape(-1, own)
    chosen = (all_times[None, :] == jnp.arange(steps)[:, None]).astype(jnp.float32)
    sum_table = jnp.dot(chosen, segs, precision=lax.Precision.HIGHEST)
    return (
        output,
        grad_start,
        sum_qkv,
        sum_out,
        sum_up,
        sum_down,
        late_sum[:own],
        late_sum[own : 2 * own],
        early[:own],
        early[own : 2 * own],
        late_sum[2 * own : 3 * own],
        late_sum[3 * own :],
        early[2 * own : 3 * own],
        early[4 * own :],
        early[3 * own : 4 * own],
        sum_table,
    )


def solution(mesh):
    in_specs = (
        P("dp", None),
        P("dp"),
        P("dp", None),
        P("dp", None),
        P("dp", None),
        P("dp", None),
        P("dp"),
        P("dp"),
        P("dp"),
        P("dp"),
        P("dp"),
        P("dp"),
        P("dp"),
        P("dp"),
        P("dp"),
        P(None, "dp"),
        P("dp", None),
    )
    out_specs = (
        P("dp", None),
        P("dp", None),
        P("dp", None),
        P("dp", None),
        P("dp", None),
        P("dp", None),
        P("dp"),
        P("dp"),
        P("dp"),
        P("dp"),
        P("dp"),
        P("dp"),
        P("dp"),
        P("dp"),
        P("dp"),
        P(None, "dp"),
    )
    return jax.shard_map(
        functools.partial(per_device, mesh.shape["dp"]), mesh=mesh, in_specs=in_specs, out_specs=out_specs, check_vma=False
    )
```

```python
import functools
import jax
import jax.numpy as jnp
from jax import lax
from jax.experimental import pallas as pl
from jax.experimental.pallas import tpu as pltpu
from jax.sharding import PartitionSpec as P

HEAD_DIM = 64
PAIR = 2 * HEAD_DIM
EPSILON = 1e-05
SCALE_FACTOR = 0.125
BF16 = jnp.bfloat16
F32 = jnp.float32
NT = (((1,), (1,)), ((), ()))
TN = (((0,), (0,)), ((), ()))


def dot(left, right, dims=(((1,), (0,)), ((), ()))):
    return lax.dot_general(left, right, dims, preferred_element_type=F32)


def normalize(hidden):
    centred = hidden - jnp.mean(hidden, axis=-1, keepdims=True)
    inverse = lax.rsqrt(jnp.mean(centred * centred, axis=-1, keepdims=True) + EPSILON)
    return centred * inverse, inverse


def norm_back(grad_out, gain, normed, inverse):
    scaled = grad_out * gain
    return inverse * (
        scaled
        - jnp.mean(scaled, axis=-1, keepdims=True)
        - normed * jnp.mean(scaled * normed, axis=-1, keepdims=True)
    )


def whole(shape):
    zeros = (0,) * len(shape)
    return pl.BlockSpec(shape, lambda *_: zeros)


def call(kernel, grid, in_specs, out_specs, out_shape, flops, scratch=(), exps=0, name=None):
    moved = sum(s.size * s.dtype.itemsize for s in out_shape) * 2
    return pl.pallas_call(
        kernel,
        grid=grid,
        in_specs=in_specs,
        out_specs=out_specs,
        out_shape=out_shape,
        scratch_shapes=list(scratch),
        compiler_params=pltpu.CompilerParams(vmem_limit_bytes=56 * 1024 * 1024),
        cost_estimate=pl.CostEstimate(flops=flops, bytes_accessed=moved, transcendentals=exps),
        name=name,
    )


GAIN_A, SHIFT_A, GAIN_F, SHIFT_F, BIAS_Q, BIAS_V, BIAS_OUT, BIAS_DOWN = range(8)
LANES = 128
TILE = 16


def pack_kernel(time_ref, table, *refs):
    vectors, up, out, held = refs[:8], refs[8], refs[9], refs[10]
    steps, own = table.shape
    held[...] = jnp.zeros_like(held)
    held[0:steps, 0:own] = table[...].astype(F32)
    for k, vector in enumerate(vectors):
        held[64 + k : 65 + k, 0:own] = vector[...]
    held[72 : 72 + up.shape[0], 0:own] = up[...]
    held[80:81, :] = jnp.full((1, LANES), time_ref[0].astype(F32))
    out[...] = held[...].T[0:own, :].astype(BF16)


def pack(timesteps, table, vectors, bias_up):
    own = table.shape[1]
    vmem = pl.BlockSpec(memory_space=pltpu.VMEM)
    return pl.pallas_call(
        pack_kernel,
        in_specs=[pl.BlockSpec(memory_space=pltpu.SMEM)] + [vmem] * 10,
        out_specs=vmem,
        out_shape=jax.ShapeDtypeStruct((own, LANES), BF16),
        scratch_shapes=[pltpu.VMEM((LANES, LANES), F32)],
        name="pack",
    )(
        timesteps,
        table,
        *[vector.astype(F32).reshape(1, own) for vector in vectors],
        bias_up.astype(F32).reshape(-1, own),
    )


def unpack_kernel(time_ref, packed, out, held):
    held[...] = packed[...].astype(F32).T
    out[0:8, :] = held[64:72, :]
    out[8:9, :] = held[pl.ds(time_ref[0], 1), :]


def unpack(timesteps, packed):
    width = packed.shape[0]
    vmem = pl.BlockSpec(memory_space=pltpu.VMEM)
    return pl.pallas_call(
        unpack_kernel,
        in_specs=[pl.BlockSpec(memory_space=pltpu.SMEM), vmem],
        out_specs=vmem,
        out_shape=jax.ShapeDtypeStruct((16, width), F32),
        scratch_shapes=[pltpu.VMEM((LANES, width), F32)],
        name="unpack",
    )(timesteps, packed)


def split_two(value):
    high = value.astype(BF16)
    return high, (value - high.astype(F32)).astype(BF16)


def in_order(source, target, places):
    for block, place in enumerate(places):
        target[block * TILE : (block + 1) * TILE, :] = source[place * TILE : (place + 1) * TILE, :]


def project_kernel(places, tok, vec, w, proj_out, turned_out, w_out):
    @pl.when(pl.program_id(0) == 0)
    def _():
        in_order(w, w_out, places)

    start = tok[...].astype(F32) + vec[8:9, :]
    normed, _ = normalize(start)
    entry = (normed * vec[GAIN_A : GAIN_A + 1, :] + vec[SHIFT_A : SHIFT_A + 1, :]).astype(BF16)
    turned_out[...] = entry.T
    product = dot(entry, w_out[...])
    width = tok.shape[1]
    proj_out[:, :width] = (product[:, :width] + vec[BIAS_Q : BIAS_Q + 1, :]).astype(BF16)
    proj_out[:, width : 2 * width] = product[:, width : 2 * width].astype(BF16)
    proj_out[:, 2 * width :] = (product[:, 2 * width :] + vec[BIAS_V : BIAS_V + 1, :]).astype(BF16)


def project(tokens, vec, w, places, block=256):
    rows, width = tokens.shape
    cols = w.shape[1]
    return call(
        functools.partial(project_kernel, places),
        (rows // block,),
        [
            pl.BlockSpec((block, width), lambda i: (i, 0)),
            whole(vec.shape),
            whole(w.shape),
        ],
        [
            pl.BlockSpec((block, cols), lambda i: (i, 0)),
            pl.BlockSpec((width, block), lambda i: (0, i)),
            whole(w.shape),
        ],
        [
            jax.ShapeDtypeStruct((rows, cols), BF16),
            jax.ShapeDtypeStruct((width, rows), BF16),
            jax.ShapeDtypeStruct(w.shape, BF16),
        ],
        2 * rows * width * cols,
        name="project",
    )(tokens, vec, w)


def attend_kernel(block, q_ref, k_ref, v_ref, mixed_out, stat_out):
    rows = q_ref.shape[0]
    first = lax.broadcasted_iota(jnp.int32, (1, PAIR), 1) < HEAD_DIM
    keys_in = k_ref[...]
    values = jnp.concatenate([v_ref[...], jnp.ones((rows, PAIR), BF16)], axis=1)
    for at in range(0, rows, block):
        queries = q_ref[at : at + block, :] * BF16(SCALE_FACTOR)
        parts = []
        for head in range(2):
            own = first if head == 0 else jnp.logical_not(first)
            scores = dot(jnp.where(own, queries, BF16(0)), keys_in, NT)
            top = jnp.max(scores, axis=1, keepdims=True)
            raised = jnp.exp(scores - top).astype(BF16)
            both = dot(raised, values)
            total = both[:, PAIR:]
            parts.append((both[:, :PAIR] / total, top + jnp.log(total)))
        mixed_out[at : at + block, :] = jnp.where(first, parts[0][0], parts[1][0]).astype(BF16)
        stat_out[at : at + block, :] = jnp.where(first, parts[1][1], parts[0][1])


def attend(proj, block=256):
    rows, cols = proj.shape
    width = cols // 3
    pairs = width // PAIR
    return call(
        functools.partial(attend_kernel, block),
        (pairs,),
        [
            pl.BlockSpec((rows, PAIR), lambda p: (0, p)),
            pl.BlockSpec((rows, PAIR), lambda p: (0, pairs + p)),
            pl.BlockSpec((rows, PAIR), lambda p: (0, 2 * pairs + p)),
        ],
        [pl.BlockSpec((rows, PAIR), lambda p: (0, p))] * 2,
        [
            jax.ShapeDtypeStruct((rows, width), BF16),
            jax.ShapeDtypeStruct((rows, width), F32),
        ],
        4 * rows * rows * width,
        exps=rows * rows * width // HEAD_DIM,
        name="attend",
    )(proj, proj, proj)


def three_parts(value):
    high = value.astype(BF16).astype(F32)
    middle = (value - high).astype(BF16).astype(F32)
    return high, middle, value - high - middle


def attend_back_kernel(
    block, q_ref, k_ref, v_ref, g_ref, mixed_ref, stat_ref, turned_ref, grad_out, weight_out, sums_out
):
    rows = q_ref.shape[0]
    lane = lax.broadcasted_iota(jnp.int32, (1, PAIR), 1)
    first = lane < HEAD_DIM
    spot = lax.rem(lane, HEAD_DIM)
    queries = q_ref[...] * BF16(SCALE_FACTOR)
    grads = g_ref[...]
    product = grads.astype(F32) * mixed_ref[...].astype(F32)
    logs = three_parts(stat_ref[...])
    minus = jnp.where(spot < 3, BF16(-1), BF16(0))

    def beside(own, value, parts):
        extra = jnp.where(
            spot == 0, parts[0], jnp.where(spot == 1, parts[1], jnp.where(spot == 2, parts[2], 0.0))
        )
        return jnp.where(own, value, extra.astype(BF16))

    grad_q = []
    grad_k = []
    grad_v = []
    heads = []
    for head in range(2):
        own = first if head == 0 else jnp.logical_not(first)
        delta = jnp.sum(jnp.where(own, product, 0.0), axis=1, keepdims=True)
        heads.append((own, beside(own, queries, logs), beside(own, grads, three_parts(delta))))
    total_q = [None, None]
    for at in range(0, rows, block):
        keys_in = k_ref[at : at + block, :]
        values = v_ref[at : at + block, :]
        out_k = []
        out_v = []
        for head, (own, queries_wide, grads_wide) in enumerate(heads):
            probs = jnp.exp(dot(jnp.where(own, keys_in, minus), queries_wide, NT))
            out_v.append(dot(probs.astype(BF16), grads))
            spread = dot(jnp.where(own, values, minus), grads_wide, NT)
            inner = (probs * spread).astype(BF16)
            out_k.append(dot(inner, queries))
            part = dot(inner, keys_in, TN)
            total_q[head] = part if total_q[head] is None else total_q[head] + part
        grad_k.append(jnp.where(first, out_k[0], out_k[1]).astype(BF16))
        grad_v.append(jnp.where(first, out_v[0], out_v[1]).astype(BF16))
    grad_q = (jnp.where(first, total_q[0], total_q[1]) * SCALE_FACTOR).astype(BF16)
    joined = jnp.concatenate(
        [grad_q, jnp.concatenate(grad_k, axis=0), jnp.concatenate(grad_v, axis=0)], axis=1
    )
    grad_out[...] = joined
    weight_out[...] = dot(turned_ref[...], joined).astype(BF16)
    sums_out[...] = jnp.sum(joined.astype(F32), axis=0, keepdims=True)


def attend_back(proj, grad_mixed, mixed, stats, turned, begin, count, block=256):
    rows, cols = proj.shape
    width = cols // 3
    pairs = width // PAIR
    column = pl.BlockSpec((rows, PAIR), lambda p: (0, begin + p))
    return call(
        functools.partial(attend_back_kernel, block),
        (count,),
        [
            column,
            pl.BlockSpec((rows, PAIR), lambda p: (0, pairs + begin + p)),
            pl.BlockSpec((rows, PAIR), lambda p: (0, 2 * pairs + begin + p)),
            column,
            column,
            column,
            whole((width, rows)),
        ],
        [
            pl.BlockSpec((rows, 3 * PAIR), lambda p: (0, p)),
            pl.BlockSpec((width, 3 * PAIR), lambda p: (0, p)),
            pl.BlockSpec((1, 3 * PAIR), lambda p: (0, p)),
        ],
        [
            jax.ShapeDtypeStruct((rows, 3 * PAIR * count), BF16),
            jax.ShapeDtypeStruct((width, 3 * PAIR * count), BF16),
            jax.ShapeDtypeStruct((1, 3 * PAIR * count), F32),
        ],
        count * (10 * rows * rows * PAIR + 6 * rows * width * PAIR),
        exps=2 * count * rows * rows,
        name="attend_back",
    )(proj, proj, proj, grad_mixed, mixed, stats, turned)


ROOT_HALF = 0.7071067811865476
ROOT_TWO_PI = 0.3989422804014327


def feed_kernel(
    places,
    tok,
    mixed,
    cot,
    joint,
    vec,
    b_up,
    output,
    grad_mid_out,
    grad_mixed_out,
    joint_out,
    sums_out,
    sums_up_out,
    w_out,
    w_up,
    w_down,
    acc_down,
    acc_up,
    acc_out,
    acc_sums,
    acc_sums_up,
):
    step = pl.program_id(0)
    bias_out, gain, shift, bias_down = (
        vec[k : k + 1, :] for k in (BIAS_OUT, GAIN_F, SHIFT_F, BIAS_DOWN)
    )
    width = tok.shape[1]
    hidden = w_up.shape[1]
    folds = hidden // width
    edge = width + hidden

    @pl.when(step == 0)
    def _():
        in_order(joint.at[:, :width], w_out, places)
        in_order(joint.at[:, width:edge], w_up, places)
        for block, place in enumerate(places):
            for fold in range(folds):
                at = (block * folds + fold) * TILE
                w_down[at : at + TILE, :] = joint[
                    place * TILE : (place + 1) * TILE, edge + fold * width : edge + (fold + 1) * width
                ]

    start = tok[...].astype(F32) + vec[8:9, :]
    middle = start + dot(mixed[...], w_out[...]) + bias_out
    normed, inverse = normalize(middle)
    entry = (normed * gain + shift).astype(BF16)
    entry_t = entry.T
    cot_now = cot[...]
    cot_t = cot_now.T
    chunk = 512
    result = middle + bias_down
    grad_feed = jnp.zeros_like(middle)

    @pl.when(step == 0)
    def _():
        acc_down[...] = jnp.zeros_like(acc_down)
        acc_up[...] = jnp.zeros_like(acc_up)
        acc_out[...] = jnp.zeros_like(acc_out)
        acc_sums[...] = jnp.zeros_like(acc_sums)
        acc_sums_up[...] = jnp.zeros_like(acc_sums_up)

    for at in range(0, hidden, chunk):
        up = w_up[:, at : at + chunk]
        down = w_down[at : at + chunk, :]
        pre = dot(entry, up) + b_up[:, at : at + chunk]
        cdf = 0.5 + 0.5 * lax.erf(pre * ROOT_HALF)
        act = (pre * cdf).astype(BF16)
        slope = cdf + pre * (ROOT_TWO_PI * jnp.exp(-0.5 * pre * pre))
        result = result + dot(act, down)
        acc_down[:, at : at + chunk] += dot(cot_t, act)
        grad_pre = (dot(cot_now, down, NT) * slope).astype(BF16)
        acc_up[:, at : at + chunk] += dot(entry_t, grad_pre)
        acc_sums_up[:, at : at + chunk] += jnp.sum(grad_pre.astype(F32), axis=0, keepdims=True)
        grad_feed = grad_feed + dot(grad_pre, up, NT)
    output[...] = result.astype(BF16)
    grad_res = cot_now.astype(F32)
    grad_mid = grad_res + norm_back(grad_feed, gain, normed, inverse)
    grad_mid_out[...] = grad_mid
    branch = grad_mid.astype(BF16)
    grad_mixed_out[...] = dot(branch, w_out[...], NT).astype(BF16)
    acc_out[...] += dot(mixed[...].T, branch)
    for k, value in enumerate((grad_feed * normed, grad_feed, branch.astype(F32), grad_res)):
        acc_sums[k : k + 1, :] += jnp.sum(value, axis=0, keepdims=True)

    @pl.when(step == pl.num_programs(0) - 1)
    def _():
        per = chunk // (TILE * folds)
        for at in range(0, hidden, chunk):
            turned = acc_down[:, at : at + chunk].astype(BF16).T
            for k in range(per):
                place = places[at // (TILE * folds) + k] * TILE
                for fold in range(folds):
                    joint_out[place : place + TILE, edge + fold * width : edge + (fold + 1) * width] = (
                        turned[(k * folds + fold) * TILE : (k * folds + fold + 1) * TILE, :]
                    )
        for block, place in enumerate(places):
            rows = slice(block * TILE, (block + 1) * TILE)
            spot = slice(place * TILE, (place + 1) * TILE)
            joint_out[spot, :width] = acc_out[rows, :].astype(BF16)
            joint_out[spot, width:edge] = acc_up[rows, :].astype(BF16)
        sums_out[...] = acc_sums[...]
        sums_up_out[...] = acc_sums_up[...]


def feed(tokens, mixed, cotangent, joint, vec, b_up, places, block=256):
    rows, width = tokens.shape
    hidden = b_up.shape[1]
    blocked = pl.BlockSpec((block, width), lambda i: (i, 0))
    return call(
        functools.partial(feed_kernel, places),
        (rows // block,),
        [blocked, blocked, blocked, whole(joint.shape), whole(vec.shape), whole(b_up.shape)],
        [
            blocked,
            blocked,
            blocked,
            whole(joint.shape),
            whole((8, width)),
            whole((1, hidden)),
        ],
        [
            jax.ShapeDtypeStruct((rows, width), BF16),
            jax.ShapeDtypeStruct((rows, width), F32),
            jax.ShapeDtypeStruct((rows, width), BF16),
            jax.ShapeDtypeStruct(joint.shape, BF16),
            jax.ShapeDtypeStruct((8, width), F32),
            jax.ShapeDtypeStruct((1, hidden), F32),
        ],
        12 * rows * width * hidden + 6 * rows * width * width,
        scratch=[
            pltpu.VMEM((width, width), BF16),
            pltpu.VMEM((width, hidden), BF16),
            pltpu.VMEM((hidden, width), BF16),
            pltpu.VMEM((width, hidden), F32),
            pltpu.VMEM((width, hidden), F32),
            pltpu.VMEM((width, width), F32),
            pltpu.VMEM((8, width), F32),
            pltpu.VMEM((1, hidden), F32),
        ],
        exps=2 * rows * hidden,
        name="feed",
    )(tokens, mixed, cotangent, joint, vec, b_up)


def finish_kernel(tok, vec, grad_mid, w, feed_sums, up_sums, proj_sums, *refs):
    grad_parts = refs[:-3]
    grad_out, sums_out, acc = refs[-3:]
    step = pl.program_id(0)
    normed, inverse = normalize(tok[...].astype(F32) + vec[8:9, :])
    grad_attn = jnp.zeros_like(normed)
    width = tok.shape[1]
    pairs = width // PAIR
    at = 0
    for part in grad_parts:
        count = part.shape[1] // (3 * PAIR)
        columns = []
        for k in range(count):
            for kind in range(3):
                column = (kind * pairs + at + k) * PAIR
                columns.append(w[:, column : column + PAIR])
        at += count
        grad_attn = grad_attn + dot(part[...], jnp.concatenate(columns, axis=1), NT)
    gain = vec[GAIN_A : GAIN_A + 1, :]
    grad_start = grad_mid[...] + norm_back(grad_attn, gain, normed, inverse)
    grad_out[...] = grad_start

    @pl.when(step == 0)
    def _():
        acc[...] = jnp.zeros_like(acc)

    for k, value in enumerate((grad_start, grad_attn * normed, grad_attn)):
        acc[k : k + 1, :] += jnp.sum(value, axis=0, keepdims=True)

    @pl.when(step == pl.num_programs(0) - 1)
    def _():
        acc[3:7, :] = feed_sums[0:4, :]
        acc[7:11, :] = up_sums[...]
        for k in range(pairs):
            acc[11:12, k * PAIR : (k + 1) * PAIR] = proj_sums[:, 3 * k * PAIR : (3 * k + 1) * PAIR]
            acc[12:13, k * PAIR : (k + 1) * PAIR] = proj_sums[
                :, (3 * k + 2) * PAIR : (3 * k + 3) * PAIR
            ]
        high, low = split_two(acc[...].T)
        half = acc.shape[0] // 2
        lane = lax.broadcasted_iota(jnp.int32, (1, acc.shape[0]), 1)
        shifted = pltpu.roll(low.astype(F32), half, 1)
        sums_out[...] = jnp.where(lane < half, high.astype(F32), shifted).astype(BF16)


def finish(tokens, vec, grad_mid, w, feed_sums, up_sums, proj_sums, grad_parts, block=256):
    rows, width = tokens.shape
    blocked = pl.BlockSpec((block, width), lambda i: (i, 0))
    return call(
        finish_kernel,
        (rows // block,),
        [
            blocked,
            whole(vec.shape),
            blocked,
            whole(w.shape),
            whole(feed_sums.shape),
            whole(up_sums.shape),
            whole(proj_sums.shape),
        ]
        + [pl.BlockSpec((block, part.shape[1]), lambda i: (i, 0)) for part in grad_parts],
        [blocked, whole((width, LANES))],
        [
            jax.ShapeDtypeStruct((rows, width), F32),
            jax.ShapeDtypeStruct((width, LANES), BF16),
        ],
        6 * rows * width * width,
        scratch=[pltpu.VMEM((LANES, width), F32)],
        name="finish",
    )(tokens, vec, grad_mid, w, feed_sums, up_sums, proj_sums, *grad_parts)


def collect_kernel(times, parts, vectors_out, table_out):
    count, own, _ = parts.shape
    lane = lax.broadcasted_iota(jnp.int32, (1, LANES), 1)
    total = jnp.zeros((own, LANES), F32)
    table = jnp.zeros((own, LANES), F32)
    for source in range(count):
        part = parts[source].astype(F32)
        part = part + pltpu.roll(part, LANES // 2, 1)
        total = total + part
        table = table + jnp.where(lane == times[source], part[:, 0:1], 0.0)
    vectors_out[...] = total.T[0:16, :]
    table_out[...] = table.T[0 : table_out.shape[0], :]


def collect(times, parts, steps):
    own = parts.shape[1]
    vmem = pl.BlockSpec(memory_space=pltpu.VMEM)
    return pl.pallas_call(
        collect_kernel,
        in_specs=[pl.BlockSpec(memory_space=pltpu.SMEM), vmem],
        out_specs=[vmem, vmem],
        out_shape=[
            jax.ShapeDtypeStruct((16, own), F32),
            jax.ShapeDtypeStruct((steps, own), F32),
        ],
        name="collect",
    )(times, parts)


def radices(count):
    sizes, rest = [2], count // 2
    while rest > 1:
        step = 4 if rest % 4 == 0 else (2 if rest % 2 == 0 else rest)
        sizes.append(step)
        rest //= step
    return sizes


def digit_groups(count, level):
    sizes = radices(count)
    stride = 1
    for size in sizes[:level]:
        stride *= size
    size = sizes[level]
    groups = []
    for base in range(count):
        if (base // stride) % size == 0:
            groups.append([base + stride * k for k in range(size)])
    return groups


def exchange(value, groups=None):
    return lax.all_to_all(value, "dp", 0, 0, tiled=True, axis_index_groups=groups)


def gather(shard, count):
    sizes = radices(count)
    value = shard
    for level in reversed(range(len(sizes))):
        spread = jnp.broadcast_to(value[None], (sizes[level],) + value.shape)
        value = exchange(spread, digit_groups(count, level))
    return value


def places_of(count):
    sizes = radices(count)
    places = []
    for device in range(count):
        place = 0
        for size in sizes:
            place = place * size + device % size
            device //= size
        places.append(place)
    return tuple(places)


def natural(value, count, lead):
    order = tuple(reversed(range(lead))) + tuple(range(lead, value.ndim))
    return value.transpose(order).reshape((count,) + value.shape[lead:])


def scatter_sum(blocks, count):
    sizes = radices(count)
    value = blocks
    for level in range(len(sizes)):
        value = jnp.sum(exchange(value, digit_groups(count, level)).astype(F32), axis=0)
        if level < len(sizes) - 1:
            value = value.astype(BF16)
    return value


def per_device(
    count,
    tokens,
    timesteps,
    w_qkv,
    w_out,
    w_up,
    w_down,
    gain_attn,
    shift_attn,
    gain_ffn,
    shift_ffn,
    bias_query,
    bias_value,
    bias_out,
    bias_up,
    bias_down,
    step_table,
    cotangent,
):
    rows, width = tokens.shape
    own = width // count
    steps = step_table.shape[0]
    hidden = w_up.shape[1]
    folds = hidden // width
    sizes = radices(count)
    lead = len(sizes)
    tiled = own == TILE
    places = places_of(count) if tiled else tuple(range(width // TILE))

    full_qkv = gather(w_qkv, count)
    if not tiled:
        full_qkv = natural(full_qkv, count, lead)
    full_qkv = full_qkv.reshape(width, -1)
    vectors = (
        gain_attn,
        shift_attn,
        gain_ffn,
        shift_ffn,
        bias_query,
        bias_value,
        bias_out,
        bias_down,
    )
    packed = pack(timesteps, step_table, vectors, bias_up)
    packed_all = exchange(jnp.broadcast_to(packed[None], (count,) + packed.shape))
    times = packed_all[:, 0, 80].astype(jnp.int32)
    up_bias = packed_all[:, :, 72 : 72 + folds].astype(F32).transpose(0, 2, 1).reshape(1, hidden)
    vec = unpack(timesteps, packed_all.reshape(width, LANES))

    joint = jnp.concatenate(
        [w_out, w_up] + [w_down[k * own : (k + 1) * own] for k in range(folds)], axis=1
    )
    joint = gather(joint, count)
    if not tiled:
        joint = natural(joint, count, lead).reshape(width, -1)
        down = joint[:, width + hidden :].reshape(count, own, folds, width)
        down = down.transpose(0, 2, 1, 3).reshape(width // TILE, folds, TILE, width)
        down = down.transpose(0, 2, 1, 3).reshape(width, hidden)
        joint = jnp.concatenate([joint[:, : width + hidden], down], axis=1)
    joint = joint.reshape(width, -1)

    proj, turned, full_qkv = project(tokens, vec, full_qkv, places)
    mixed, stats = attend(proj)
    output, grad_mid, grad_mixed, grad_joint, feed_sums, up_sums = feed(
        tokens, mixed, cotangent, joint, vec, up_bias, places
    )
    if not tiled:
        down = grad_joint[:, width + hidden :].reshape(width // TILE, TILE, folds, width)
        down = down.transpose(0, 2, 1, 3).reshape(count, folds, own, width)
        down = down.transpose(0, 2, 1, 3).reshape(width, hidden)
        grad_joint = jnp.concatenate([grad_joint[:, : width + hidden], down], axis=1)
        grad_joint = grad_joint.reshape(tuple(reversed(sizes)) + (own, -1))
        grad_joint = grad_joint.transpose(tuple(reversed(range(lead))) + (lead, lead + 1))
    grad_joint = grad_joint.reshape(tuple(sizes) + (own, -1))
    sum_joint = scatter_sum(grad_joint, count)

    pairs = width // PAIR
    grad_parts, weight_sums, proj_sums = [], [], []
    for begin, number in ((0, pairs // 2), (pairs // 2, pairs - pairs // 2)):
        grad_part, weight_part, part_sums = attend_back(
            proj, grad_mixed, mixed, stats, turned, begin, number
        )
        grad_parts.append(grad_part)
        proj_sums.append(part_sums)
        weight_part = exchange(weight_part.reshape(count, own, -1))
        weight_sums.append(jnp.sum(weight_part.astype(F32), axis=0))

    turned_sums = up_sums.reshape(count, folds, own).transpose(1, 0, 2).reshape(folds, width)
    grad_start, packed_sums = finish(
        tokens,
        vec,
        grad_mid,
        full_qkv,
        feed_sums,
        turned_sums,
        jnp.concatenate(proj_sums, axis=1),
        grad_parts,
    )
    sums, sum_table = collect(times, exchange(packed_sums.reshape(count, own, LANES)), steps)

    weight = jnp.concatenate(weight_sums, axis=1)
    sum_qkv = jnp.concatenate(
        [
            weight[:, (3 * pair + kind) * PAIR : (3 * pair + kind + 1) * PAIR]
            for kind in range(3)
            for pair in range(pairs)
        ],
        axis=1,
    )
    edge = width + hidden
    sum_down = jnp.concatenate(
        [sum_joint[:, edge + k * width : edge + (k + 1) * width] for k in range(folds)], axis=0
    )
    return (
        output,
        grad_start,
        sum_qkv,
        sum_joint[:, :width],
        sum_joint[:, width:edge],
        sum_down,
        sums[1],
        sums[2],
        sums[3],
        sums[4],
        sums[11],
        sums[12],
        sums[5],
        sums[7:11].reshape(-1),
        sums[6],
        sum_table,
    )


def solution(mesh):
    in_specs = (
        P("dp", None),
        P("dp"),
        P("dp", None),
        P("dp", None),
        P("dp", None),
        P("dp", None),
        P("dp"),
        P("dp"),
        P("dp"),
        P("dp"),
        P("dp"),
        P("dp"),
        P("dp"),
        P("dp"),
        P("dp"),
        P(None, "dp"),
        P("dp", None),
    )
    out_specs = (
        P("dp", None),
        P("dp", None),
        P("dp", None),
        P("dp", None),
        P("dp", None),
        P("dp", None),
        P("dp"),
        P("dp"),
        P("dp"),
        P("dp"),
        P("dp"),
        P("dp"),
        P("dp"),
        P("dp"),
        P("dp"),
        P(None, "dp"),
    )
    return jax.shard_map(
        functools.partial(per_device, mesh.shape["dp"]), mesh=mesh, in_specs=in_specs, out_specs=out_specs, check_vma=False
    )
```

```python
import functools
import jax
import jax.numpy as jnp
from jax import lax
from jax.experimental import pallas as pl
from jax.experimental.pallas import tpu as pltpu
from jax.sharding import PartitionSpec as P

HEAD_DIM = 64
PAIR = 2 * HEAD_DIM
EPSILON = 1e-05
SCALE_FACTOR = 0.125
BF16 = jnp.bfloat16
F32 = jnp.float32
NT = (((1,), (1,)), ((), ()))
TN = (((0,), (0,)), ((), ()))


def dot(left, right, dims=(((1,), (0,)), ((), ()))):
    return lax.dot_general(left, right, dims, preferred_element_type=F32)


def normalize(hidden):
    centred = hidden - jnp.mean(hidden, axis=-1, keepdims=True)
    inverse = lax.rsqrt(jnp.mean(centred * centred, axis=-1, keepdims=True) + EPSILON)
    return centred * inverse, inverse


def norm_back(grad_out, gain, normed, inverse):
    scaled = grad_out * gain
    return inverse * (
        scaled
        - jnp.mean(scaled, axis=-1, keepdims=True)
        - normed * jnp.mean(scaled * normed, axis=-1, keepdims=True)
    )


def whole(shape):
    zeros = (0,) * len(shape)
    return pl.BlockSpec(shape, lambda *_: zeros)


def call(kernel, grid, in_specs, out_specs, out_shape, flops, scratch=(), exps=0, name=None):
    moved = sum(s.size * s.dtype.itemsize for s in out_shape) * 2
    return pl.pallas_call(
        kernel,
        grid=grid,
        in_specs=in_specs,
        out_specs=out_specs,
        out_shape=out_shape,
        scratch_shapes=list(scratch),
        compiler_params=pltpu.CompilerParams(vmem_limit_bytes=56 * 1024 * 1024),
        cost_estimate=pl.CostEstimate(flops=flops, bytes_accessed=moved, transcendentals=exps),
        name=name,
    )


GAIN_A, SHIFT_A, GAIN_F, SHIFT_F, BIAS_Q, BIAS_V, BIAS_OUT, BIAS_DOWN = range(8)
LANES = 128
TILE = 16


def pack_kernel(time_ref, w, table, *refs):
    vectors, up, out, held = refs[:8], refs[8], refs[9], refs[10]
    own, steps = table.shape
    cols = w.shape[1]
    held[...] = jnp.zeros_like(held)
    for k, vector in enumerate(vectors):
        held[64 + k : 65 + k, 0:own] = vector[...].astype(F32).reshape(1, own)
    wide = up[...].astype(F32).reshape(1, up.shape[0])
    for k in range(up.shape[0] // own):
        held[72 + k : 73 + k, 0:own] = wide[:, k * own : (k + 1) * own]
    held[80:81, :] = jnp.full((1, LANES), time_ref[0].astype(F32))
    packed = held[...].T[0:own, :].astype(BF16)
    out[:, 0:cols] = w[...]
    out[:, cols:] = packed
    out[:, cols : cols + steps] = table[...]


def pack(timesteps, w, table, vectors, bias_up):
    own, cols = w.shape
    vmem = pl.BlockSpec(memory_space=pltpu.VMEM)
    return pl.pallas_call(
        pack_kernel,
        in_specs=[pl.BlockSpec(memory_space=pltpu.SMEM)] + [vmem] * 11,
        out_specs=vmem,
        out_shape=jax.ShapeDtypeStruct((own, cols + LANES), BF16),
        scratch_shapes=[pltpu.VMEM((LANES, LANES), F32)],
        name="pack",
    )(timesteps, w, table.T, *vectors, bias_up)


def split_two(value):
    high = value.astype(BF16)
    return high, (value - high.astype(F32)).astype(BF16)


def rows_at(block, fold=1):
    return pl.ds(pl.multiple_of(block * (TILE * fold), TILE * fold), TILE * fold)


def in_order(me, sources, apart, columns, target):
    for source, steps in zip(sources, apart):
        for block, step in enumerate(steps):
            target[rows_at(me ^ step), :] = source[block * TILE : (block + 1) * TILE, columns]


def project_kernel(apart, me_ref, time_ref, tok, *refs):
    sources = refs[: len(apart)]
    proj_out, turned_out, w_out, vec, small_out, held = refs[len(apart) :]
    cols = w_out.shape[1]

    @pl.when(pl.program_id(0) == 0)
    def _():
        me = me_ref[0]
        in_order(me, sources, apart, slice(0, cols), w_out)
        in_order(me, sources, apart, slice(cols, cols + LANES), small_out)
        held[...] = small_out[...].astype(F32).T
        vec[0:8, :] = held[64:72, :]
        vec[8:9, :] = held[pl.ds(time_ref[0], 1), :]
        vec[9:16, :] = jnp.zeros((7, vec.shape[1]), F32)

    start = tok[...].astype(F32) + vec[8:9, :]
    normed, _ = normalize(start)
    entry = (normed * vec[GAIN_A : GAIN_A + 1, :] + vec[SHIFT_A : SHIFT_A + 1, :]).astype(BF16)
    turned_out[...] = entry.T
    product = dot(entry, w_out[...])
    width = tok.shape[1]
    proj_out[:, :width] = (product[:, :width] + vec[BIAS_Q : BIAS_Q + 1, :]).astype(BF16)
    proj_out[:, width : 2 * width] = product[:, width : 2 * width].astype(BF16)
    proj_out[:, 2 * width :] = (product[:, 2 * width :] + vec[BIAS_V : BIAS_V + 1, :]).astype(BF16)


def project(me, timesteps, tokens, sources, apart, block=256):
    rows, width = tokens.shape
    cols = sources[0].shape[1] - LANES
    smem = pl.BlockSpec(memory_space=pltpu.SMEM)
    return call(
        functools.partial(project_kernel, apart),
        (rows // block,),
        [
            smem,
            smem,
            pl.BlockSpec((block, width), lambda i: (i, 0)),
        ]
        + [whole(source.shape) for source in sources],
        [
            pl.BlockSpec((block, cols), lambda i: (i, 0)),
            pl.BlockSpec((width, block), lambda i: (0, i)),
            whole((width, cols)),
            whole((16, width)),
            whole((width, LANES)),
        ],
        [
            jax.ShapeDtypeStruct((rows, cols), BF16),
            jax.ShapeDtypeStruct((width, rows), BF16),
            jax.ShapeDtypeStruct((width, cols), BF16),
            jax.ShapeDtypeStruct((16, width), F32),
            jax.ShapeDtypeStruct((width, LANES), BF16),
        ],
        2 * rows * width * cols,
        scratch=[pltpu.VMEM((LANES, width), F32)],
        name="project",
    )(me, timesteps, tokens, *sources)


def attend_kernel(block, q_ref, k_ref, v_ref, mixed_out, stat_out):
    rows = q_ref.shape[0]
    first = lax.broadcasted_iota(jnp.int32, (1, PAIR), 1) < HEAD_DIM
    keys_in = k_ref[...]
    values = jnp.concatenate([v_ref[...], jnp.ones((rows, PAIR), BF16)], axis=1)
    for at in range(0, rows, block):
        queries = q_ref[at : at + block, :] * BF16(SCALE_FACTOR)
        parts = []
        for head in range(2):
            own = first if head == 0 else jnp.logical_not(first)
            scores = dot(jnp.where(own, queries, BF16(0)), keys_in, NT)
            top = jnp.max(scores, axis=1, keepdims=True)
            raised = jnp.exp(scores - top).astype(BF16)
            both = dot(raised, values)
            total = both[:, PAIR:]
            parts.append((both[:, :PAIR] / total, top + jnp.log(total)))
        mixed_out[at : at + block, :] = jnp.where(first, parts[0][0], parts[1][0]).astype(BF16)
        stat_out[at : at + block, :] = jnp.where(first, parts[1][1], parts[0][1])


def attend(proj, block=256):
    rows, cols = proj.shape
    width = cols // 3
    pairs = width // PAIR
    return call(
        functools.partial(attend_kernel, block),
        (pairs,),
        [
            pl.BlockSpec((rows, PAIR), lambda p: (0, p)),
            pl.BlockSpec((rows, PAIR), lambda p: (0, pairs + p)),
            pl.BlockSpec((rows, PAIR), lambda p: (0, 2 * pairs + p)),
        ],
        [pl.BlockSpec((rows, PAIR), lambda p: (0, p))] * 2,
        [
            jax.ShapeDtypeStruct((rows, width), BF16),
            jax.ShapeDtypeStruct((rows, width), F32),
        ],
        4 * rows * rows * width,
        exps=rows * rows * width // HEAD_DIM,
        name="attend",
    )(proj, proj, proj)


def three_parts(value):
    high = value.astype(BF16).astype(F32)
    middle = (value - high).astype(BF16).astype(F32)
    return high, middle, value - high - middle


def attend_back_kernel(
    block, leaving, me_ref, q_ref, k_ref, v_ref, g_ref, mixed_ref, stat_ref, turned_ref, *refs
):
    grad_out, sums_out = refs[:2]
    targets = refs[2 : 2 + len(leaving)]
    held = refs[-1]
    rows = q_ref.shape[0]
    lane = lax.broadcasted_iota(jnp.int32, (1, PAIR), 1)
    first = lane < HEAD_DIM
    spot = lax.rem(lane, HEAD_DIM)
    queries = q_ref[...] * BF16(SCALE_FACTOR)
    grads = g_ref[...]
    product = grads.astype(F32) * mixed_ref[...].astype(F32)
    logs = three_parts(stat_ref[...])
    minus = jnp.where(spot < 3, BF16(-1), BF16(0))

    def beside(own, value, parts):
        extra = jnp.where(
            spot == 0, parts[0], jnp.where(spot == 1, parts[1], jnp.where(spot == 2, parts[2], 0.0))
        )
        return jnp.where(own, value, extra.astype(BF16))

    grad_q = []
    grad_k = []
    grad_v = []
    heads = []
    for head in range(2):
        own = first if head == 0 else jnp.logical_not(first)
        delta = jnp.sum(jnp.where(own, product, 0.0), axis=1, keepdims=True)
        heads.append((own, beside(own, queries, logs), beside(own, grads, three_parts(delta))))
    total_q = [None, None]
    for at in range(0, rows, block):
        keys_in = k_ref[at : at + block, :]
        values = v_ref[at : at + block, :]
        out_k = []
        out_v = []
        for head, (own, queries_wide, grads_wide) in enumerate(heads):
            probs = jnp.exp(dot(jnp.where(own, keys_in, minus), queries_wide, NT))
            out_v.append(dot(probs.astype(BF16), grads))
            spread = dot(jnp.where(own, values, minus), grads_wide, NT)
            inner = (probs * spread).astype(BF16)
            out_k.append(dot(inner, queries))
            part = dot(inner, keys_in, TN)
            total_q[head] = part if total_q[head] is None else total_q[head] + part
        grad_k.append(jnp.where(first, out_k[0], out_k[1]).astype(BF16))
        grad_v.append(jnp.where(first, out_v[0], out_v[1]).astype(BF16))
    grad_q = (jnp.where(first, total_q[0], total_q[1]) * SCALE_FACTOR).astype(BF16)
    joined = jnp.concatenate(
        [grad_q, jnp.concatenate(grad_k, axis=0), jnp.concatenate(grad_v, axis=0)], axis=1
    )
    grad_out[...] = joined
    held[...] = dot(turned_ref[...], joined).astype(BF16)
    me = me_ref[0]
    for target, steps in zip(targets, leaving):
        for place, step in enumerate(steps):
            target[place * TILE : (place + 1) * TILE, :] = held[rows_at(me ^ step), :]
    sums_out[...] = jnp.sum(joined.astype(F32), axis=0, keepdims=True)


def attend_back(me, leaving, proj, grad_mixed, mixed, stats, turned, begin, count, block=256):
    rows, cols = proj.shape
    width = cols // 3
    pairs = width // PAIR
    column = pl.BlockSpec((rows, PAIR), lambda p: (0, begin + p))
    return call(
        functools.partial(attend_back_kernel, block, leaving),
        (count,),
        [
            pl.BlockSpec(memory_space=pltpu.SMEM),
            column,
            pl.BlockSpec((rows, PAIR), lambda p: (0, pairs + begin + p)),
            pl.BlockSpec((rows, PAIR), lambda p: (0, 2 * pairs + begin + p)),
            column,
            column,
            column,
            whole((width, rows)),
        ],
        [
            pl.BlockSpec((rows, 3 * PAIR), lambda p: (0, p)),
            pl.BlockSpec((1, 3 * PAIR), lambda p: (0, p)),
        ]
        + [pl.BlockSpec((len(steps) * TILE, 3 * PAIR), lambda p: (0, p)) for steps in leaving],
        [
            jax.ShapeDtypeStruct((rows, 3 * PAIR * count), BF16),
            jax.ShapeDtypeStruct((1, 3 * PAIR * count), F32),
        ]
        + [jax.ShapeDtypeStruct((len(steps) * TILE, 3 * PAIR * count), BF16) for steps in leaving],
        count * (10 * rows * rows * PAIR + 6 * rows * width * PAIR),
        scratch=[pltpu.VMEM((width, 3 * PAIR), BF16)],
        exps=2 * count * rows * rows,
        name="attend_back",
    )(me, proj, proj, proj, grad_mixed, mixed, stats, turned)


ROOT_HALF = 0.7071067811865476
ROOT_TWO_PI = 0.3989422804014327


def feed_kernel(
    apart,
    leaving,
    me_ref,
    tok,
    mixed,
    cot,
    vec,
    b_up,
    *refs,
):
    sources = refs[: len(apart)]
    refs = refs[len(apart) :]
    output, grad_mid_out, grad_mixed_out = refs[:3]
    targets = refs[3 : 3 + len(leaving)]
    (
        sums_out,
        sums_up_out,
        w_out,
        w_up,
        w_down,
        acc_down,
        acc_up,
        acc_out,
        acc_sums,
        acc_sums_up,
    ) = refs[3 + len(leaving) :]
    step = pl.program_id(0)
    bias_out, gain, shift, bias_down = (
        vec[k : k + 1, :] for k in (BIAS_OUT, GAIN_F, SHIFT_F, BIAS_DOWN)
    )
    width = tok.shape[1]
    hidden = w_up.shape[1]
    folds = hidden // width
    edge = width + hidden
    me = me_ref[0]

    @pl.when(step == 0)
    def _():
        in_order(me, sources, apart, slice(0, width), w_out)
        in_order(me, sources, apart, slice(width, edge), w_up)
        for source, steps in zip(sources, apart):
            for block, far in enumerate(steps):
                for fold in range(folds):
                    w_down[rows_at((me ^ far) * folds + fold), :] = source[
                        block * TILE : (block + 1) * TILE,
                        edge + fold * width : edge + (fold + 1) * width,
                    ]

    start = tok[...].astype(F32) + vec[8:9, :]
    middle = start + dot(mixed[...], w_out[...]) + bias_out
    normed, inverse = normalize(middle)
    entry = (normed * gain + shift).astype(BF16)
    entry_t = entry.T
    cot_now = cot[...]
    cot_t = cot_now.T
    chunk = 512
    result = middle + bias_down
    grad_feed = jnp.zeros_like(middle)

    @pl.when(step == 0)
    def _():
        acc_down[...] = jnp.zeros_like(acc_down)
        acc_up[...] = jnp.zeros_like(acc_up)
        acc_out[...] = jnp.zeros_like(acc_out)
        acc_sums[...] = jnp.zeros_like(acc_sums)
        acc_sums_up[...] = jnp.zeros_like(acc_sums_up)

    for at in range(0, hidden, chunk):
        up = w_up[:, at : at + chunk]
        down = w_down[at : at + chunk, :]
        pre = dot(entry, up) + b_up[:, at : at + chunk]
        cdf = 0.5 + 0.5 * lax.erf(pre * ROOT_HALF)
        act = (pre * cdf).astype(BF16)
        slope = cdf + pre * (ROOT_TWO_PI * jnp.exp(-0.5 * pre * pre))
        result = result + dot(act, down)
        acc_down[:, at : at + chunk] += dot(cot_t, act)
        grad_pre = (dot(cot_now, down, NT) * slope).astype(BF16)
        acc_up[:, at : at + chunk] += dot(entry_t, grad_pre)
        acc_sums_up[:, at : at + chunk] += jnp.sum(grad_pre.astype(F32), axis=0, keepdims=True)
        grad_feed = grad_feed + dot(grad_pre, up, NT)
    output[...] = result.astype(BF16)
    grad_res = cot_now.astype(F32)
    grad_mid = grad_res + norm_back(grad_feed, gain, normed, inverse)
    grad_mid_out[...] = grad_mid
    branch = grad_mid.astype(BF16)
    grad_mixed_out[...] = dot(branch, w_out[...], NT).astype(BF16)
    acc_out[...] += dot(mixed[...].T, branch)
    for k, value in enumerate((grad_feed * normed, grad_feed, branch.astype(F32), grad_res)):
        acc_sums[k : k + 1, :] += jnp.sum(value, axis=0, keepdims=True)

    @pl.when(step == pl.num_programs(0) - 1)
    def _():
        for at in range(0, hidden, chunk):
            w_down[at : at + chunk, :] = acc_down[:, at : at + chunk].astype(BF16).T
        for target, steps in zip(targets, leaving):
            for block, far in enumerate(steps):
                spot = slice(block * TILE, (block + 1) * TILE)
                source = me ^ far
                target[spot, :width] = acc_out[rows_at(source), :].astype(BF16)
                target[spot, width:edge] = acc_up[rows_at(source), :].astype(BF16)
                for fold in range(folds):
                    target[spot, edge + fold * width : edge + (fold + 1) * width] = w_down[
                        rows_at(source * folds + fold), :
                    ]
        sums_out[...] = acc_sums[...]
        sums_up_out[...] = acc_sums_up[...]


def feed(me, tokens, mixed, cotangent, sources, apart, leaving, vec, b_up, block=256):
    rows, width = tokens.shape
    hidden = b_up.shape[1]
    columns = sources[0].shape[1]
    blocked = pl.BlockSpec((block, width), lambda i: (i, 0))
    return call(
        functools.partial(feed_kernel, apart, leaving),
        (rows // block,),
        [
            pl.BlockSpec(memory_space=pltpu.SMEM),
            blocked,
            blocked,
            blocked,
            whole(vec.shape),
            whole(b_up.shape),
        ]
        + [whole(source.shape) for source in sources],
        [
            blocked,
            blocked,
            blocked,
        ]
        + [whole((len(steps) * TILE, columns)) for steps in leaving]
        + [
            whole((8, width)),
            whole((1, hidden)),
        ],
        [
            jax.ShapeDtypeStruct((rows, width), BF16),
            jax.ShapeDtypeStruct((rows, width), F32),
            jax.ShapeDtypeStruct((rows, width), BF16),
        ]
        + [jax.ShapeDtypeStruct((len(steps) * TILE, columns), BF16) for steps in leaving]
        + [
            jax.ShapeDtypeStruct((8, width), F32),
            jax.ShapeDtypeStruct((1, hidden), F32),
        ],
        12 * rows * width * hidden + 6 * rows * width * width,
        scratch=[
            pltpu.VMEM((width, width), BF16),
            pltpu.VMEM((width, hidden), BF16),
            pltpu.VMEM((hidden, width), BF16),
            pltpu.VMEM((width, hidden), F32),
            pltpu.VMEM((width, hidden), F32),
            pltpu.VMEM((width, width), F32),
            pltpu.VMEM((8, width), F32),
            pltpu.VMEM((1, hidden), F32),
        ],
        exps=2 * rows * hidden,
        name="feed",
    )(me, tokens, mixed, cotangent, vec, b_up, *sources)


def finish_kernel(tok, vec, grad_mid, w, feed_sums, up_sums, proj_sums, *refs):
    grad_parts = refs[:-3]
    grad_out, sums_out, acc = refs[-3:]
    step = pl.program_id(0)
    normed, inverse = normalize(tok[...].astype(F32) + vec[8:9, :])
    grad_attn = jnp.zeros_like(normed)
    width = tok.shape[1]
    pairs = width // PAIR
    at = 0
    for part in grad_parts:
        count = part.shape[1] // (3 * PAIR)
        columns = []
        for k in range(count):
            for kind in range(3):
                column = (kind * pairs + at + k) * PAIR
                columns.append(w[:, column : column + PAIR])
        at += count
        grad_attn = grad_attn + dot(part[...], jnp.concatenate(columns, axis=1), NT)
    gain = vec[GAIN_A : GAIN_A + 1, :]
    grad_start = grad_mid[...] + norm_back(grad_attn, gain, normed, inverse)
    grad_out[...] = grad_start

    @pl.when(step == 0)
    def _():
        acc[...] = jnp.zeros_like(acc)

    for k, value in enumerate((grad_start, grad_attn * normed, grad_attn)):
        acc[k : k + 1, :] += jnp.sum(value, axis=0, keepdims=True)

    @pl.when(step == pl.num_programs(0) - 1)
    def _():
        acc[3:7, :] = feed_sums[0:4, :]
        acc[7:11, :] = up_sums[...]
        for k in range(pairs):
            acc[11:12, k * PAIR : (k + 1) * PAIR] = proj_sums[:, 3 * k * PAIR : (3 * k + 1) * PAIR]
            acc[12:13, k * PAIR : (k + 1) * PAIR] = proj_sums[
                :, (3 * k + 2) * PAIR : (3 * k + 3) * PAIR
            ]
        high, low = split_two(acc[...].T)
        half = acc.shape[0] // 2
        lane = lax.broadcasted_iota(jnp.int32, (1, acc.shape[0]), 1)
        shifted = pltpu.roll(low.astype(F32), half, 1)
        sums_out[...] = jnp.where(lane < half, high.astype(F32), shifted).astype(BF16)


def finish(tokens, vec, grad_mid, w, feed_sums, up_sums, proj_sums, grad_parts, block=256):
    rows, width = tokens.shape
    blocked = pl.BlockSpec((block, width), lambda i: (i, 0))
    return call(
        finish_kernel,
        (rows // block,),
        [
            blocked,
            whole(vec.shape),
            blocked,
            whole(w.shape),
            whole(feed_sums.shape),
            whole(up_sums.shape),
            whole(proj_sums.shape),
        ]
        + [pl.BlockSpec((block, part.shape[1]), lambda i: (i, 0)) for part in grad_parts],
        [blocked, whole((width, LANES))],
        [
            jax.ShapeDtypeStruct((rows, width), F32),
            jax.ShapeDtypeStruct((width, LANES), BF16),
        ],
        6 * rows * width * width,
        scratch=[pltpu.VMEM((LANES, width), F32)],
        name="finish",
    )(tokens, vec, grad_mid, w, feed_sums, up_sums, proj_sums, *grad_parts)


def collect_kernel(times, parts, vectors_out, table_out):
    count, own, _ = parts.shape
    lane = lax.broadcasted_iota(jnp.int32, (1, LANES), 1)
    total = jnp.zeros((own, LANES), F32)
    table = jnp.zeros((own, LANES), F32)
    for source in range(count):
        part = parts[source].astype(F32)
        part = part + pltpu.roll(part, LANES // 2, 1)
        total = total + part
        table = table + jnp.where(lane == times[source], part[:, 0:1], 0.0)
    vectors_out[...] = total.T[0:16, :]
    table_out[...] = table[:, 0 : table_out.shape[1]]


def collect(times, parts, steps):
    own = parts.shape[1]
    vmem = pl.BlockSpec(memory_space=pltpu.VMEM)
    return pl.pallas_call(
        collect_kernel,
        in_specs=[pl.BlockSpec(memory_space=pltpu.SMEM), vmem],
        out_specs=[vmem, vmem],
        out_shape=[
            jax.ShapeDtypeStruct((16, own), F32),
            jax.ShapeDtypeStruct((own, steps), F32),
        ],
        name="collect",
    )(times, parts)


def levels_of(count):
    bits = (count - 1).bit_length()
    if count != 1 << bits:
        raise ValueError("device count")
    return [[0]] + [list(range(at, min(at + 2, bits))) for at in range(1, bits, 2)]


def masks_of(bits):
    return [step << bits[0] for step in range(1 << len(bits))]


def permute(value, mask, count):
    return lax.ppermute(value, "dp", [(device, device ^ mask) for device in range(count)])


def gather_level(value, bits, count):
    return [value] + [permute(value, mask, count) for mask in masks_of(bits)[1:]]


def total(parts):
    result = parts[0].astype(F32)
    for part in parts[1:]:
        result = result + part.astype(F32)
    return result


def reduce_level(pieces, bits, count):
    return [pieces[0]] + [
        permute(piece, mask, count) for piece, mask in zip(pieces[1:], masks_of(bits)[1:])
    ]


def fold_down(rows, folds, own, back):
    width = rows.shape[1] // folds
    old, new = (TILE, own) if back else (own, TILE)
    rows = rows.reshape(-1, old, folds, width).transpose(0, 2, 1, 3)
    rows = rows.reshape(-1, folds, new, width).transpose(0, 2, 1, 3)
    return rows.reshape(-1, folds * width)


def refold(value, folded, folds, own, back):
    if not folded:
        return value
    edge = value.shape[1] - folded
    return jnp.concatenate([value[:, :edge], fold_down(value[:, edge:], folds, own, back)], axis=1)


class Plan:
    def __init__(self, count, own, folds):
        self.count, self.own, self.folds = count, own, folds
        self.levels = levels_of(count)
        self.tiled = own == TILE and len(self.levels) == 3
        index = lax.axis_index("dp").astype(jnp.int32)
        if self.tiled:
            near, middle, far = (masks_of(bits) for bits in self.levels)
            self.apart = tuple(
                tuple(a + b + c for c in far) for a in near for b in middle
            )
            self.leaving = tuple(tuple(a + b + c for b in middle for c in far) for a in near)
            self.me = index.reshape(1)
        else:
            self.index = index
            self.apart = self.leaving = (tuple(range(own * count // TILE)),)
            self.me = jnp.zeros((1,), jnp.int32)

    def spread(self, shard, level):
        return gather_level(shard, self.levels[level], self.count)

    def near(self, halves):
        keep, send = halves
        return keep, permute(send, 1, self.count)

    def cut(self, parts):
        size = parts[0].shape[0] // 4
        return [
            total([part[k * size : (k + 1) * size] for part in parts]).astype(BF16)
            for k in range(4)
        ]

    def middle(self, parts):
        return self.cut(parts)

    def around(self, pieces):
        return reduce_level(pieces, self.levels[1], self.count)

    def finish(self, parts):
        return total(reduce_level(self.cut(parts), self.levels[2], self.count))

    def whole(self, shard, folded):
        value = shard
        for bits in reversed(self.levels):
            value = jnp.stack(gather_level(value, bits, self.count))
        value = value.reshape((self.count,) + shard.shape)
        value = value[self.places() ^ self.place(self.index)]
        return refold(value.reshape(-1, shard.shape[1]), folded, self.folds, self.own, False)

    def place(self, device):
        result = 0
        for bits in self.levels:
            result = (result << len(bits)) | ((device >> bits[0]) & ((1 << len(bits)) - 1))
        return result

    def places(self):
        return self.place(jnp.arange(self.count, dtype=jnp.int32))

    def sum_whole(self, value, folded):
        value = refold(value, folded, self.folds, self.own, True)
        value = value.reshape(self.count, self.own, -1)
        order = [0] * self.count
        for device in range(self.count):
            order[self.place(device)] = device
        value = value[jnp.array(order, jnp.int32) ^ self.index]
        for at, bits in enumerate(self.levels):
            value = value.reshape((1 << len(bits), -1) + value.shape[1:])
            value = total(reduce_level(list(value), bits, self.count))
            if at < len(self.levels) - 1:
                value = value.astype(BF16)
        return value.reshape(self.own, -1)


def exchange(value):
    return lax.all_to_all(value, "dp", 0, 0, tiled=True)


def per_device(
    count,
    tokens,
    timesteps,
    w_qkv,
    w_out,
    w_up,
    w_down,
    gain_attn,
    shift_attn,
    gain_ffn,
    shift_ffn,
    bias_query,
    bias_value,
    bias_out,
    bias_up,
    bias_down,
    step_table,
    cotangent,
):
    rows, width = tokens.shape
    own = width // count
    steps = step_table.shape[0]
    hidden = w_up.shape[1]
    folds = hidden // width
    edge = width + hidden
    plan = Plan(count, own, folds)
    pairs = width // PAIR

    vectors = (
        gain_attn,
        shift_attn,
        gain_ffn,
        shift_ffn,
        bias_query,
        bias_value,
        bias_out,
        bias_down,
    )
    entry = pack(timesteps, w_qkv, step_table, vectors, bias_up)
    joint = jnp.concatenate(
        [w_out, w_up] + [w_down[k * own : (k + 1) * own] for k in range(folds)], axis=1
    )
    if plan.tiled:
        entry = jnp.concatenate(plan.spread(entry, 2), axis=0)
        entry, joint = lax.optimization_barrier((entry, joint))
        entries = plan.spread(entry, 1)
        joint = jnp.concatenate(plan.spread(joint, 2), axis=0)
        *entries, joint = lax.optimization_barrier((*entries, joint))
        entries = entries + [permute(entry, 1, count) for entry in entries]
        joints = plan.spread(joint, 1)
    else:
        entries = [plan.whole(entry, 0)]
        joints = [plan.whole(joint, hidden)]

    proj, turned, full_qkv, vec, small = project(
        plan.me, timesteps, tokens, entries, plan.apart
    )
    small = small.reshape(count, own, LANES)
    times = small[:, 0, 80].astype(jnp.int32)
    up_bias = small[:, :, 72 : 72 + folds].astype(F32).transpose(0, 2, 1).reshape(1, hidden)
    mixed, stats = attend(proj)

    if plan.tiled:
        joints = joints + [permute(joint, 1, count) for joint in joints]
    feed_out = feed(
        plan.me, tokens, mixed, cotangent, joints, plan.apart, plan.leaving, vec, up_bias
    )
    output, grad_mid, grad_mixed = feed_out[:3]
    feed_sums, up_sums = feed_out[-2:]
    grad_parts, proj_sums, weights = [], [], []

    def back(begin, number):
        grad_part, part_sums, *weight_parts = attend_back(
            plan.me, plan.leaving, proj, grad_mixed, mixed, stats, turned, begin, number
        )
        grad_parts.append(grad_part)
        proj_sums.append(part_sums)
        return weight_parts

    if plan.tiled:
        work = plan.near(feed_out[3:5])
        first = back(0, 1)
        work, grad_mixed = lax.optimization_barrier((plan.middle(work), grad_mixed))
        work = plan.around(work)
        second = back(1, pairs - 2)
        second = plan.near(second)
        third = back(pairs - 1, 1)
        third = plan.near(third)
        first = plan.near(first)
        sum_joint = plan.finish(work)
        weights = [plan.finish(plan.around(plan.middle(part))) for part in (first, second, third)]
    else:
        sum_joint = plan.sum_whole(feed_out[3], hidden)
        weights = [plan.sum_whole(back(0, pairs)[0], 0)]
    weight = jnp.concatenate(weights, axis=1)

    turned_sums = up_sums.reshape(count, folds, own).transpose(1, 0, 2).reshape(folds, width)
    grad_start, packed_sums = finish(
        tokens,
        vec,
        grad_mid,
        full_qkv,
        feed_sums,
        turned_sums,
        jnp.concatenate(proj_sums, axis=1),
        grad_parts,
    )
    sums, sum_table = collect(times, exchange(packed_sums.reshape(count, own, LANES)), steps)

    sum_qkv = jnp.concatenate(
        [
            weight[:, (3 * pair + kind) * PAIR : (3 * pair + kind + 1) * PAIR]
            for kind in range(3)
            for pair in range(pairs)
        ],
        axis=1,
    )
    sum_down = jnp.concatenate(
        [sum_joint[:, edge + k * width : edge + (k + 1) * width] for k in range(folds)], axis=0
    )
    return (
        output,
        grad_start,
        sum_qkv,
        sum_joint[:, :width],
        sum_joint[:, width:edge],
        sum_down,
        sums[1],
        sums[2],
        sums[3],
        sums[4],
        sums[11],
        sums[12],
        sums[5],
        sums[7:11].reshape(-1),
        sums[6],
        sum_table.T,
    )


def solution(mesh):
    in_specs = (
        P("dp", None),
        P("dp"),
        P("dp", None),
        P("dp", None),
        P("dp", None),
        P("dp", None),
        P("dp"),
        P("dp"),
        P("dp"),
        P("dp"),
        P("dp"),
        P("dp"),
        P("dp"),
        P("dp"),
        P("dp"),
        P(None, "dp"),
        P("dp", None),
    )
    out_specs = (
        P("dp", None),
        P("dp", None),
        P("dp", None),
        P("dp", None),
        P("dp", None),
        P("dp", None),
        P("dp"),
        P("dp"),
        P("dp"),
        P("dp"),
        P("dp"),
        P("dp"),
        P("dp"),
        P("dp"),
        P("dp"),
        P(None, "dp"),
    )
    return jax.shard_map(
        functools.partial(per_device, mesh.shape["dp"]), mesh=mesh, in_specs=in_specs, out_specs=out_specs, check_vma=False
    )
```

```python
import functools
import jax
import jax.numpy as jnp
from jax import lax
from jax.experimental import pallas as pl
from jax.experimental.pallas import tpu as pltpu
from jax.sharding import PartitionSpec as P

HEAD_DIM = 64
PAIR = 2 * HEAD_DIM
EPSILON = 1e-05
SCALE_FACTOR = 0.125
BF16 = jnp.bfloat16
F32 = jnp.float32
NT = (((1,), (1,)), ((), ()))
TN = (((0,), (0,)), ((), ()))


def dot(left, right, dims=(((1,), (0,)), ((), ()))):
    return lax.dot_general(left, right, dims, preferred_element_type=F32)


def normalize(hidden):
    centred = hidden - jnp.mean(hidden, axis=-1, keepdims=True)
    inverse = lax.rsqrt(jnp.mean(centred * centred, axis=-1, keepdims=True) + EPSILON)
    return centred * inverse, inverse


def norm_back(grad_out, gain, normed, inverse):
    scaled = grad_out * gain
    return inverse * (
        scaled
        - jnp.mean(scaled, axis=-1, keepdims=True)
        - normed * jnp.mean(scaled * normed, axis=-1, keepdims=True)
    )


def whole(shape):
    zeros = (0,) * len(shape)
    return pl.BlockSpec(shape, lambda *_: zeros)


def call(kernel, grid, in_specs, out_specs, out_shape, flops, scratch=(), exps=0, name=None, aliases=None):
    moved = sum(s.size * s.dtype.itemsize for s in out_shape) * 2
    return pl.pallas_call(
        kernel,
        grid=grid,
        in_specs=in_specs,
        out_specs=out_specs,
        out_shape=out_shape,
        scratch_shapes=list(scratch),
        input_output_aliases=aliases or {},
        compiler_params=pltpu.CompilerParams(vmem_limit_bytes=56 * 1024 * 1024),
        cost_estimate=pl.CostEstimate(flops=flops, bytes_accessed=moved, transcendentals=exps),
        name=name,
    )


GAIN_A, SHIFT_A, GAIN_F, SHIFT_F, BIAS_Q, BIAS_V, BIAS_OUT, BIAS_DOWN = range(8)
LANES = 128
TILE = 16


def pack_kernel(w, table, *refs):
    vectors, up, out, held = refs[:8], refs[8], refs[9], refs[10]
    own, steps = table.shape
    cols = w.shape[1]
    held[...] = jnp.zeros_like(held)
    for k, vector in enumerate(vectors):
        held[64 + k : 65 + k, 0:own] = vector[...].astype(F32).reshape(1, own)
    wide = up[...].astype(F32).reshape(1, up.shape[0])
    for k in range(up.shape[0] // own):
        held[72 + k : 73 + k, 0:own] = wide[:, k * own : (k + 1) * own]
    packed = held[...].T[0:own, :].astype(BF16)
    out[:, 0:cols] = w[...]
    out[:, cols:] = packed
    out[:, cols : cols + steps] = table[...]


def pack(w, table, vectors, bias_up):
    own, cols = w.shape
    vmem = pl.BlockSpec(memory_space=pltpu.VMEM)
    return pl.pallas_call(
        pack_kernel,
        in_specs=[vmem] * 11,
        out_specs=vmem,
        out_shape=jax.ShapeDtypeStruct((own, cols + LANES), BF16),
        scratch_shapes=[pltpu.VMEM((LANES, LANES), F32)],
        name="pack",
    )(w, table.T, *vectors, bias_up)


def join_kernel(w_out, w_up, w_down, out):
    own, width = w_out.shape
    edge = width + w_up.shape[1]
    out[:, 0:width] = w_out[...]
    out[:, width:edge] = w_up[...]
    for fold in range(w_down.shape[0] // own):
        out[:, edge + fold * width : edge + (fold + 1) * width] = w_down[fold * own : (fold + 1) * own, :]


def join(w_out, w_up, w_down):
    own, width = w_out.shape
    columns = width + w_up.shape[1] + w_down.shape[0] // own * width
    vmem = pl.BlockSpec(memory_space=pltpu.VMEM)
    return pl.pallas_call(
        join_kernel,
        in_specs=[vmem] * 3,
        out_specs=vmem,
        out_shape=jax.ShapeDtypeStruct((own, columns), BF16),
        name="join",
    )(w_out, w_up, w_down)


def folded_place(own, folds, fold, shape, feature_axis):
    feature = lax.broadcasted_iota(jnp.int32, shape, feature_axis)
    unit = lax.broadcasted_iota(jnp.int32, shape, 1 - feature_axis)
    device = lax.div(feature, own)
    place = device * (own * folds) + fold * own + (feature - device * own)
    return jnp.where(unit == place, 1.0, 0.0).astype(BF16)


def split_two(value):
    high = value.astype(BF16)
    return high, (value - high.astype(F32)).astype(BF16)


def rows_at(block, fold=1):
    return pl.ds(pl.multiple_of(block * (TILE * fold), TILE * fold), TILE * fold)


def in_order(me, sources, apart, columns, target):
    for source, steps in zip(sources, apart):
        for block, step in enumerate(steps):
            target[rows_at(me ^ step), :] = source[block * TILE : (block + 1) * TILE, columns]


def project_kernel(apart, own, folds, me_ref, time_ref, tok, *refs):
    sources = refs[: len(apart)]
    proj_out, turned_out, w_out, vec, b_up, small, held = refs[len(apart) :]
    cols = w_out.shape[1]

    @pl.when(pl.program_id(0) == 0)
    def _():
        me = me_ref[0]
        in_order(me, sources, apart, slice(0, cols), w_out)
        in_order(me, sources, apart, slice(cols, cols + LANES), small)
        held[...] = small[...].astype(F32).T
        vec[0:8, :] = held[64:72, :]
        vec[8:9, :] = held[pl.ds(time_ref[0], 1), :]
        vec[9:16, :] = jnp.full((7, vec.shape[1]), time_ref[0].astype(F32))
        wide = jnp.zeros(b_up.shape, F32)
        for fold in range(folds):
            row = held[72 + fold : 73 + fold, :]
            rows = [row[:, at : at + LANES] for at in range(0, row.shape[1], LANES)]
            rows = jnp.concatenate(rows + rows, axis=0)[0:8].astype(BF16)
            wide = wide + dot(rows, folded_place(own, folds, fold, (LANES, LANES * folds), 0))
        b_up[...] = wide

    start = tok[...].astype(F32) + vec[8:9, :]
    normed, _ = normalize(start)
    entry = (normed * vec[GAIN_A : GAIN_A + 1, :] + vec[SHIFT_A : SHIFT_A + 1, :]).astype(BF16)
    turned_out[...] = entry.T
    product = dot(entry, w_out[...])
    width = tok.shape[1]
    proj_out[:, :width] = (product[:, :width] + vec[BIAS_Q : BIAS_Q + 1, :]).astype(BF16)
    proj_out[:, width : 2 * width] = product[:, width : 2 * width].astype(BF16)
    proj_out[:, 2 * width :] = (product[:, 2 * width :] + vec[BIAS_V : BIAS_V + 1, :]).astype(BF16)


def project(me, timesteps, tokens, sources, apart, own, folds, block=256):
    rows, width = tokens.shape
    cols = sources[0].shape[1] - LANES
    smem = pl.BlockSpec(memory_space=pltpu.SMEM)
    return call(
        functools.partial(project_kernel, apart, own, folds),
        (rows // block,),
        [
            smem,
            smem,
            pl.BlockSpec((block, width), lambda i: (i, 0)),
        ]
        + [whole(source.shape) for source in sources],
        [
            pl.BlockSpec((block, cols), lambda i: (i, 0)),
            pl.BlockSpec((width, block), lambda i: (0, i)),
            whole((width, cols)),
            whole((16, width)),
            whole((8, LANES * folds)),
        ],
        [
            jax.ShapeDtypeStruct((rows, cols), BF16),
            jax.ShapeDtypeStruct((width, rows), BF16),
            jax.ShapeDtypeStruct((width, cols), BF16),
            jax.ShapeDtypeStruct((16, width), F32),
            jax.ShapeDtypeStruct((8, LANES * folds), F32),
        ],
        2 * rows * width * cols,
        scratch=[pltpu.VMEM((width, LANES), BF16), pltpu.VMEM((LANES, width), F32)],
        name="project",
    )(me, timesteps, tokens, *sources)


def attend_kernel(block, q_ref, k_ref, v_ref, mixed_out, stat_out):
    rows = q_ref.shape[0]
    first = lax.broadcasted_iota(jnp.int32, (1, PAIR), 1) < HEAD_DIM
    keys_in = k_ref[...]
    values = jnp.concatenate([v_ref[...], jnp.ones((rows, PAIR), BF16)], axis=1)
    for at in range(0, rows, block):
        queries = q_ref[at : at + block, :] * BF16(SCALE_FACTOR)
        parts = []
        for head in range(2):
            own = first if head == 0 else jnp.logical_not(first)
            scores = dot(jnp.where(own, queries, BF16(0)), keys_in, NT)
            top = jnp.max(scores, axis=1, keepdims=True)
            raised = jnp.exp(scores - top).astype(BF16)
            both = dot(raised, values)
            total = both[:, PAIR:]
            parts.append((both[:, :PAIR] / total, top + jnp.log(total)))
        mixed_out[at : at + block, :] = jnp.where(first, parts[0][0], parts[1][0]).astype(BF16)
        stat_out[at : at + block, :] = jnp.where(first, parts[1][1], parts[0][1])


def attend(proj, block=256):
    rows, cols = proj.shape
    width = cols // 3
    pairs = width // PAIR
    return call(
        functools.partial(attend_kernel, block),
        (pairs,),
        [
            pl.BlockSpec((rows, PAIR), lambda p: (0, p)),
            pl.BlockSpec((rows, PAIR), lambda p: (0, pairs + p)),
            pl.BlockSpec((rows, PAIR), lambda p: (0, 2 * pairs + p)),
        ],
        [pl.BlockSpec((rows, PAIR), lambda p: (0, p))] * 2,
        [
            jax.ShapeDtypeStruct((rows, width), BF16),
            jax.ShapeDtypeStruct((rows, width), F32),
        ],
        4 * rows * rows * width,
        exps=rows * rows * width // HEAD_DIM,
        name="attend",
    )(proj, proj, proj)


def three_parts(value):
    high = value.astype(BF16).astype(F32)
    middle = (value - high).astype(BF16).astype(F32)
    return high, middle, value - high - middle


def attend_back_kernel(
    block, leaving, kept, me_ref, q_ref, k_ref, v_ref, g_ref, mixed_ref, stat_ref, turned_ref, *refs
):
    refs = refs[kept:]
    grad_out, sums_out = refs[:2]
    targets = refs[2 : 2 + len(leaving)]
    held = refs[-1]
    rows = q_ref.shape[0]
    lane = lax.broadcasted_iota(jnp.int32, (1, PAIR), 1)
    first = lane < HEAD_DIM
    spot = lax.rem(lane, HEAD_DIM)
    queries = q_ref[...] * BF16(SCALE_FACTOR)
    grads = g_ref[...]
    product = grads.astype(F32) * mixed_ref[...].astype(F32)
    logs = three_parts(stat_ref[...])
    minus = jnp.where(spot < 3, BF16(-1), BF16(0))

    def beside(own, value, parts):
        extra = jnp.where(
            spot == 0, parts[0], jnp.where(spot == 1, parts[1], jnp.where(spot == 2, parts[2], 0.0))
        )
        return jnp.where(own, value, extra.astype(BF16))

    grad_q = []
    grad_k = []
    grad_v = []
    heads = []
    for head in range(2):
        own = first if head == 0 else jnp.logical_not(first)
        delta = jnp.sum(jnp.where(own, product, 0.0), axis=1, keepdims=True)
        heads.append((own, beside(own, queries, logs), beside(own, grads, three_parts(delta))))
    total_q = [None, None]
    for at in range(0, rows, block):
        keys_in = k_ref[at : at + block, :]
        values = v_ref[at : at + block, :]
        out_k = []
        out_v = []
        for head, (own, queries_wide, grads_wide) in enumerate(heads):
            probs = jnp.exp(dot(jnp.where(own, keys_in, minus), queries_wide, NT))
            out_v.append(dot(probs.astype(BF16), grads))
            spread = dot(jnp.where(own, values, minus), grads_wide, NT)
            inner = (probs * spread).astype(BF16)
            out_k.append(dot(inner, queries))
            part = dot(inner, keys_in, TN)
            total_q[head] = part if total_q[head] is None else total_q[head] + part
        grad_k.append(jnp.where(first, out_k[0], out_k[1]).astype(BF16))
        grad_v.append(jnp.where(first, out_v[0], out_v[1]).astype(BF16))
    grad_q = (jnp.where(first, total_q[0], total_q[1]) * SCALE_FACTOR).astype(BF16)
    joined = jnp.concatenate(
        [grad_q, jnp.concatenate(grad_k, axis=0), jnp.concatenate(grad_v, axis=0)], axis=1
    )
    grad_out[...] = joined
    held[...] = dot(turned_ref[...], joined).astype(BF16)
    me = me_ref[0]
    for target, steps in zip(targets, leaving):
        for place, step in enumerate(steps):
            target[place * TILE : (place + 1) * TILE, :] = held[rows_at(me ^ step), :]
    sums_out[...] = jnp.sum(joined.astype(F32), axis=0, keepdims=True)


def attend_back(me, leaving, proj, grad_mixed, mixed, stats, turned, begin, count, before=(), block=256):
    rows, cols = proj.shape
    width = cols // 3
    pairs = width // PAIR
    column = pl.BlockSpec((rows, PAIR), lambda p: (0, begin + p))
    place = lambda p: (0, begin + p)
    tall = [len(steps) * TILE for steps in leaving]
    inputs = (me, proj, proj, proj, grad_mixed, mixed, stats, turned)
    return call(
        functools.partial(attend_back_kernel, block, leaving, len(before)),
        (count,),
        [
            pl.BlockSpec(memory_space=pltpu.SMEM),
            column,
            pl.BlockSpec((rows, PAIR), lambda p: (0, pairs + begin + p)),
            pl.BlockSpec((rows, PAIR), lambda p: (0, 2 * pairs + begin + p)),
            column,
            column,
            column,
            whole((width, rows)),
        ]
        + [pl.BlockSpec(memory_space=pl.ANY)] * len(before),
        [pl.BlockSpec((rows, 3 * PAIR), place), pl.BlockSpec((1, 3 * PAIR), place)]
        + [pl.BlockSpec((high, 3 * PAIR), place) for high in tall],
        [jax.ShapeDtypeStruct((rows, cols), BF16), jax.ShapeDtypeStruct((1, cols), F32)]
        + [jax.ShapeDtypeStruct((high, cols), BF16) for high in tall],
        count * (10 * rows * rows * PAIR + 6 * rows * width * PAIR),
        scratch=[pltpu.VMEM((width, 3 * PAIR), BF16)],
        exps=2 * count * rows * rows,
        name="attend_back",
        aliases={len(inputs) + k: k for k in range(len(before))},
    )(*inputs, *before)


ROOT_HALF = 0.7071067811865476
ROOT_TWO_PI = 0.3989422804014327


def feed_kernel(
    apart,
    leaving,
    me_ref,
    tok,
    mixed,
    cot,
    vec,
    b_up,
    *refs,
):
    sources = refs[: len(apart)]
    refs = refs[len(apart) :]
    output, grad_mid_out, grad_mixed_out = refs[:3]
    targets = refs[3 : 3 + len(leaving)]
    (
        sums_out,
        sums_up_out,
        w_out,
        w_up,
        w_down,
        acc_down,
        acc_up,
        acc_out,
        acc_sums,
        acc_sums_up,
    ) = refs[3 + len(leaving) :]
    step = pl.program_id(0)
    bias_out, gain, shift, bias_down = (
        vec[k : k + 1, :] for k in (BIAS_OUT, GAIN_F, SHIFT_F, BIAS_DOWN)
    )
    width = tok.shape[1]
    hidden = w_up.shape[1]
    folds = hidden // width
    edge = width + hidden
    me = me_ref[0]

    @pl.when(step == 0)
    def _():
        in_order(me, sources, apart, slice(0, width), w_out)
        in_order(me, sources, apart, slice(width, edge), w_up)
        for source, steps in zip(sources, apart):
            for block, far in enumerate(steps):
                for fold in range(folds):
                    w_down[rows_at((me ^ far) * folds + fold), :] = source[
                        block * TILE : (block + 1) * TILE,
                        edge + fold * width : edge + (fold + 1) * width,
                    ]

    start = tok[...].astype(F32) + vec[8:9, :]
    middle = start + dot(mixed[...], w_out[...]) + bias_out
    normed, inverse = normalize(middle)
    entry = (normed * gain + shift).astype(BF16)
    entry_t = entry.T
    cot_now = cot[...]
    cot_t = cot_now.T
    chunk = b_up.shape[1]
    result = middle + bias_down
    grad_feed = jnp.zeros_like(middle)

    @pl.when(step == 0)
    def _():
        acc_down[...] = jnp.zeros_like(acc_down)
        acc_up[...] = jnp.zeros_like(acc_up)
        acc_out[...] = jnp.zeros_like(acc_out)
        acc_sums[...] = jnp.zeros_like(acc_sums)
        acc_sums_up[...] = jnp.zeros_like(acc_sums_up)

    for at in range(0, hidden, chunk):
        up = w_up[:, at : at + chunk]
        down = w_down[at : at + chunk, :]
        row = at // chunk
        pre = dot(entry, up) + b_up[row : row + 1, :]
        cdf = 0.5 + 0.5 * lax.erf(pre * ROOT_HALF)
        act = (pre * cdf).astype(BF16)
        slope = cdf + pre * (ROOT_TWO_PI * jnp.exp(-0.5 * pre * pre))
        result = result + dot(act, down)
        acc_down[:, at : at + chunk] += dot(cot_t, act)
        grad_pre = (dot(cot_now, down, NT) * slope).astype(BF16)
        acc_up[:, at : at + chunk] += dot(entry_t, grad_pre)
        acc_sums_up[row : row + 1, :] += jnp.sum(grad_pre.astype(F32), axis=0, keepdims=True)
        grad_feed = grad_feed + dot(grad_pre, up, NT)
    output[...] = result.astype(BF16)
    grad_res = cot_now.astype(F32)
    grad_mid = grad_res + norm_back(grad_feed, gain, normed, inverse)
    grad_mid_out[...] = grad_mid
    branch = grad_mid.astype(BF16)
    grad_mixed_out[...] = dot(branch, w_out[...], NT).astype(BF16)
    acc_out[...] += dot(mixed[...].T, branch)
    for k, value in enumerate((grad_feed * normed, grad_feed, branch.astype(F32), grad_res)):
        acc_sums[k : k + 1, :] += jnp.sum(value, axis=0, keepdims=True)

    @pl.when(step == pl.num_programs(0) - 1)
    def _():
        for at in range(0, hidden, chunk):
            w_down[at : at + chunk, :] = acc_down[:, at : at + chunk].astype(BF16).T
        for target, steps in zip(targets, leaving):
            for block, far in enumerate(steps):
                spot = slice(block * TILE, (block + 1) * TILE)
                source = me ^ far
                target[spot, :width] = acc_out[rows_at(source), :].astype(BF16)
                target[spot, width:edge] = acc_up[rows_at(source), :].astype(BF16)
                for fold in range(folds):
                    target[spot, edge + fold * width : edge + (fold + 1) * width] = w_down[
                        rows_at(source * folds + fold), :
                    ]
        sums_out[...] = acc_sums[...]
        sums_up_out[...] = acc_sums_up[...]


def feed(me, tokens, mixed, cotangent, sources, apart, leaving, vec, b_up, block=256):
    rows, width = tokens.shape
    columns = sources[0].shape[1]
    hidden = (columns - width) // 2
    blocked = pl.BlockSpec((block, width), lambda i: (i, 0))
    return call(
        functools.partial(feed_kernel, apart, leaving),
        (rows // block,),
        [
            pl.BlockSpec(memory_space=pltpu.SMEM),
            blocked,
            blocked,
            blocked,
            whole(vec.shape),
            whole(b_up.shape),
        ]
        + [whole(source.shape) for source in sources],
        [
            blocked,
            blocked,
            blocked,
        ]
        + [whole((len(steps) * TILE, columns)) for steps in leaving]
        + [
            whole((8, width)),
            whole(b_up.shape),
        ],
        [
            jax.ShapeDtypeStruct((rows, width), BF16),
            jax.ShapeDtypeStruct((rows, width), F32),
            jax.ShapeDtypeStruct((rows, width), BF16),
        ]
        + [jax.ShapeDtypeStruct((len(steps) * TILE, columns), BF16) for steps in leaving]
        + [
            jax.ShapeDtypeStruct((8, width), F32),
            jax.ShapeDtypeStruct(b_up.shape, F32),
        ],
        12 * rows * width * hidden + 6 * rows * width * width,
        scratch=[
            pltpu.VMEM((width, width), BF16),
            pltpu.VMEM((width, hidden), BF16),
            pltpu.VMEM((hidden, width), BF16),
            pltpu.VMEM((width, hidden), F32),
            pltpu.VMEM((width, hidden), F32),
            pltpu.VMEM((width, width), F32),
            pltpu.VMEM((8, width), F32),
            pltpu.VMEM(b_up.shape, F32),
        ],
        exps=2 * rows * hidden,
        name="feed",
    )(me, tokens, mixed, cotangent, vec, b_up, *sources)


def finish_kernel(own, tok, vec, grad_mid, w, feed_sums, up_sums, proj_sums, grad_proj, grad_out, sums_out, acc):
    step = pl.program_id(0)
    normed, inverse = normalize(tok[...].astype(F32) + vec[8:9, :])
    width = tok.shape[1]
    pairs = width // PAIR
    folds = up_sums.shape[1] // LANES
    columns = [w[:, (kind * pairs + k) * PAIR : (kind * pairs + k + 1) * PAIR] for k in range(pairs) for kind in range(3)]
    grad_attn = dot(grad_proj[...], jnp.concatenate(columns, axis=1), NT)
    gain = vec[GAIN_A : GAIN_A + 1, :]
    grad_start = grad_mid[...] + norm_back(grad_attn, gain, normed, inverse)
    grad_out[...] = grad_start

    @pl.when(step == 0)
    def _():
        acc[...] = jnp.zeros_like(acc)

    for k, value in enumerate((grad_start, grad_attn * normed, grad_attn)):
        acc[k : k + 1, :] += jnp.sum(value, axis=0, keepdims=True)

    @pl.when(step == pl.num_programs(0) - 1)
    def _():
        acc[3:7, :] = feed_sums[0:4, :]
        up_high, up_low = split_two(up_sums[...])
        for fold in range(folds):
            place = folded_place(own, folds, fold, (LANES * folds, LANES), 1)
            rows = dot(up_high, place) + dot(up_low, place)
            for k in range(width // LANES):
                acc[7 + fold : 8 + fold, k * LANES : (k + 1) * LANES] = rows[k : k + 1, :]
        for k in range(pairs):
            acc[11:12, k * PAIR : (k + 1) * PAIR] = proj_sums[:, 3 * k * PAIR : (3 * k + 1) * PAIR]
            acc[12:13, k * PAIR : (k + 1) * PAIR] = proj_sums[
                :, (3 * k + 2) * PAIR : (3 * k + 3) * PAIR
            ]
        acc[TIME : TIME + 1, :] = vec[9:10, :]
        high, low = split_two(acc[...].T)
        half = acc.shape[0] // 2
        lane = lax.broadcasted_iota(jnp.int32, (1, acc.shape[0]), 1)
        shifted = pltpu.roll(low.astype(F32), half, 1)
        sums_out[...] = jnp.where(lane < half, high.astype(F32), shifted).astype(BF16)


TIME = 13


def finish(own, tokens, vec, grad_mid, w, feed_sums, up_sums, proj_sums, grad_proj, block=256):
    rows, width = tokens.shape
    blocked = pl.BlockSpec((block, width), lambda i: (i, 0))
    return call(
        functools.partial(finish_kernel, own),
        (rows // block,),
        [
            blocked,
            whole(vec.shape),
            blocked,
            whole(w.shape),
            whole(feed_sums.shape),
            whole(up_sums.shape),
            whole(proj_sums.shape),
            pl.BlockSpec((block, grad_proj.shape[1]), lambda i: (i, 0)),
        ],
        [blocked, whole((width, LANES))],
        [
            jax.ShapeDtypeStruct((rows, width), F32),
            jax.ShapeDtypeStruct((width, LANES), BF16),
        ],
        6 * rows * width * width,
        scratch=[pltpu.VMEM((LANES, width), F32)],
        name="finish",
    )(tokens, vec, grad_mid, w, feed_sums, up_sums, proj_sums, grad_proj)


SUM_ROWS = (1, 2, 3, 4, 11, 12, 5, 6)


def collect_kernel(folds, parts, *refs):
    vectors, up, table_out, held = refs[:-3], refs[-3], refs[-2], refs[-1]
    count, own, _ = parts.shape
    lane = lax.broadcasted_iota(jnp.int32, (1, LANES), 1).astype(F32)
    total = jnp.zeros((own, LANES), F32)
    table = jnp.zeros((own, LANES), F32)
    for source in range(count):
        part = parts[source].astype(F32)
        part = part + pltpu.roll(part, LANES // 2, 1)
        total = total + part
        table = table + jnp.where(lane == part[:, TIME : TIME + 1], part[:, 0:1], 0.0)
    held[...] = jnp.zeros_like(held)
    held[0:own, :] = total
    turned = held[...].T
    for k, out in zip(SUM_ROWS, vectors):
        out[...] = turned[k, 0:own]
    wide = turned[7:8, :]
    for fold in range(1, folds):
        wide = wide + pltpu.roll(turned[7 + fold : 8 + fold, :], fold * own, 1)
    up[...] = wide[0, 0 : folds * own]
    table_out[...] = table[:, 0 : table_out.shape[1]]


def collect(parts, steps, folds):
    own = parts.shape[1]
    vmem = pl.BlockSpec(memory_space=pltpu.VMEM)
    return pl.pallas_call(
        functools.partial(collect_kernel, folds),
        in_specs=[vmem],
        out_specs=[vmem] * 10,
        out_shape=[jax.ShapeDtypeStruct((own,), F32)] * 8
        + [jax.ShapeDtypeStruct((own * folds,), F32), jax.ShapeDtypeStruct((own, steps), F32)],
        scratch_shapes=[pltpu.VMEM((LANES, LANES), F32)],
        name="collect",
    )(parts)


def settle_kernel(count, *refs):
    parts, outs = refs[:count], refs[count:]
    value = parts[0][...].astype(F32)
    for part in parts[1:]:
        value = value + part[...].astype(F32)
    own = value.shape[0]
    if len(outs) == 1:
        pairs = value.shape[1] // (3 * PAIR)
        for pair in range(pairs):
            for kind in range(3):
                at = (3 * pair + kind) * PAIR
                spot = (kind * pairs + pair) * PAIR
                outs[0][:, spot : spot + PAIR] = value[:, at : at + PAIR]
    else:
        w_out, w_up, w_down = outs
        width = w_out.shape[1]
        edge = width + w_up.shape[1]
        w_out[...] = value[:, :width]
        w_up[...] = value[:, width:edge]
        for fold in range(w_down.shape[0] // own):
            w_down[fold * own : (fold + 1) * own, :] = value[:, edge + fold * width : edge + (fold + 1) * width]


def settle(parts, shapes, name):
    vmem = pl.BlockSpec(memory_space=pltpu.VMEM)
    return pl.pallas_call(
        functools.partial(settle_kernel, len(parts)),
        in_specs=[vmem] * len(parts),
        out_specs=[vmem] * len(shapes),
        out_shape=[jax.ShapeDtypeStruct(shape, F32) for shape in shapes],
        name=name,
    )(*parts)


def levels_of(count):
    bits = (count - 1).bit_length()
    if count != 1 << bits:
        raise ValueError("device count")
    return [[0]] + [list(range(at, min(at + 2, bits))) for at in range(1, bits, 2)]


def masks_of(bits):
    return [step << bits[0] for step in range(1 << len(bits))]


def permute(value, mask, count):
    return lax.ppermute(value, "dp", [(device, device ^ mask) for device in range(count)])


def gather_level(value, bits, count):
    return [value] + [permute(value, mask, count) for mask in masks_of(bits)[1:]]


def total(parts):
    result = parts[0].astype(F32)
    for part in parts[1:]:
        result = result + part.astype(F32)
    return result


def reduce_level(pieces, bits, count):
    return [pieces[0]] + [
        permute(piece, mask, count) for piece, mask in zip(pieces[1:], masks_of(bits)[1:])
    ]


def fold_down(rows, folds, own, back):
    width = rows.shape[1] // folds
    old, new = (TILE, own) if back else (own, TILE)
    rows = rows.reshape(-1, old, folds, width).transpose(0, 2, 1, 3)
    rows = rows.reshape(-1, folds, new, width).transpose(0, 2, 1, 3)
    return rows.reshape(-1, folds * width)


def refold(value, folded, folds, own, back):
    if not folded:
        return value
    edge = value.shape[1] - folded
    return jnp.concatenate([value[:, :edge], fold_down(value[:, edge:], folds, own, back)], axis=1)


class Plan:
    def __init__(self, count, own, folds):
        self.count, self.own, self.folds = count, own, folds
        self.levels = levels_of(count)
        self.tiled = own == TILE and len(self.levels) == 3
        index = lax.axis_index("dp").astype(jnp.int32)
        if self.tiled:
            near, middle, far = (masks_of(bits) for bits in self.levels)
            self.apart = tuple(
                tuple(a + b + c for c in far) for a in near for b in middle
            )
            self.leaving = tuple(tuple(a + b + c for b in middle for c in far) for a in near)
            self.me = index.reshape(1)
        else:
            self.index = index
            self.apart = self.leaving = (tuple(range(own * count // TILE)),)
            self.me = jnp.zeros((1,), jnp.int32)

    def spread(self, shard, level):
        return gather_level(shard, self.levels[level], self.count)

    def near(self, halves):
        keep, send = halves
        return keep, permute(send, 1, self.count)

    def cut(self, parts):
        size = parts[0].shape[0] // 4
        return [
            total([part[k * size : (k + 1) * size] for part in parts]).astype(BF16)
            for k in range(4)
        ]

    def around(self, pieces):
        return reduce_level(pieces, self.levels[1], self.count)

    def far(self, pieces):
        return reduce_level(pieces, self.levels[2], self.count)

    def whole(self, shard, folded):
        value = shard
        for bits in reversed(self.levels):
            value = jnp.stack(gather_level(value, bits, self.count))
        value = value.reshape((self.count,) + shard.shape)
        value = value[self.places() ^ self.place(self.index)]
        return refold(value.reshape(-1, shard.shape[1]), folded, self.folds, self.own, False)

    def place(self, device):
        result = 0
        for bits in self.levels:
            result = (result << len(bits)) | ((device >> bits[0]) & ((1 << len(bits)) - 1))
        return result

    def places(self):
        return self.place(jnp.arange(self.count, dtype=jnp.int32))

    def sum_whole(self, value, folded):
        value = refold(value, folded, self.folds, self.own, True)
        value = value.reshape(self.count, self.own, -1)
        order = [0] * self.count
        for device in range(self.count):
            order[self.place(device)] = device
        value = value[jnp.array(order, jnp.int32) ^ self.index]
        for at, bits in enumerate(self.levels):
            value = value.reshape((1 << len(bits), -1) + value.shape[1:])
            value = total(reduce_level(list(value), bits, self.count))
            if at < len(self.levels) - 1:
                value = value.astype(BF16)
        return value.reshape(self.own, -1)


def after(value, *done):
    leaves, tree = jax.tree.flatten(value)
    return jax.tree.unflatten(tree, lax.optimization_barrier((*leaves, *done))[: len(leaves)])


def exchange(value):
    return lax.all_to_all(value, "dp", 0, 0, tiled=True)


def per_device(
    count,
    tokens,
    timesteps,
    w_qkv,
    w_out,
    w_up,
    w_down,
    gain_attn,
    shift_attn,
    gain_ffn,
    shift_ffn,
    bias_query,
    bias_value,
    bias_out,
    bias_up,
    bias_down,
    step_table,
    cotangent,
):
    rows, width = tokens.shape
    own = width // count
    steps = step_table.shape[0]
    hidden = w_up.shape[1]
    folds = hidden // width
    edge = width + hidden
    plan = Plan(count, own, folds)
    pairs = width // PAIR

    vectors = (
        gain_attn,
        shift_attn,
        gain_ffn,
        shift_ffn,
        bias_query,
        bias_value,
        bias_out,
        bias_down,
    )
    entry = pack(w_qkv, step_table, vectors, bias_up)
    if plan.tiled:
        joint = join(w_out, w_up, w_down)
        far = plan.spread(entry, 2)
        joint = plan.spread(joint, 2)
        entry = jnp.concatenate(far, axis=0)
        entries = plan.spread(entry, 1)
        joint = jnp.concatenate(after(joint, *entries[1:]), axis=0)
        entries = entries + [permute(entry, 1, count) for entry in entries]
        joints = plan.spread(joint, 1)
    else:
        joint = jnp.concatenate(
            [w_out, w_up] + [w_down[k * own : (k + 1) * own] for k in range(folds)], axis=1
        )
        entries = [plan.whole(entry, 0)]
        joints = [plan.whole(joint, hidden)]

    proj, turned, full_qkv, vec, up_bias = project(
        plan.me, timesteps, tokens, entries, plan.apart, own, folds
    )
    mixed, stats = attend(proj)

    if plan.tiled:
        joints = after(joints, mixed)
        joints = joints + [permute(joint, 1, count) for joint in joints]
    feed_out = feed(
        plan.me, tokens, mixed, cotangent, joints, plan.apart, plan.leaving, vec, up_bias
    )
    output, grad_mid, grad_mixed = feed_out[:3]
    feed_sums, up_sums = feed_out[-2:]

    def back(grad_mixed, begin, number, before=()):
        return attend_back(
            plan.me, plan.leaving, proj, grad_mixed, mixed, stats, turned, begin, number, before
        )

    if plan.tiled:
        near = plan.near(feed_out[3:5])
        first = back(grad_mixed, 0, 1)
        pieces = plan.cut(after(near, first[0]))
        grad_proj, proj_sums, *leaving = back(after(grad_mixed, *pieces), 1, pairs - 1, first)
        pieces = plan.cut(after(plan.around(pieces), grad_proj))
        near = plan.near(leaving)
        grad_mid = after(grad_mid, *pieces)
        sum_parts = plan.far(pieces)
    else:
        grad_proj, proj_sums, leaving = back(grad_mixed, 0, pairs)
        sum_parts = [plan.sum_whole(feed_out[3], hidden)]
        weight_parts = [plan.sum_whole(leaving, 0)]

    grad_start, packed_sums = finish(
        own, tokens, vec, grad_mid, full_qkv, feed_sums, up_sums, proj_sums, grad_proj
    )
    parts = exchange(packed_sums.reshape(count, own, LANES))
    if plan.tiled:
        pieces = plan.around(plan.cut(after(near, grad_start)))
        weight_parts = plan.far(plan.cut(pieces))
    *sums, sum_up, sum_table = collect(parts, steps, folds)
    sum_out, sum_w_up, sum_down = settle(
        sum_parts, (w_out.shape, w_up.shape, w_down.shape), "settle_joint"
    )
    (sum_qkv,) = settle(weight_parts, (w_qkv.shape,), "settle_qkv")
    return (
        output,
        grad_start,
        sum_qkv,
        sum_out,
        sum_w_up,
        sum_down,
        *sums[:7],
        sum_up,
        sums[7],
        sum_table.T,
    )


def solution(mesh):
    in_specs = (
        P("dp", None),
        P("dp"),
        P("dp", None),
        P("dp", None),
        P("dp", None),
        P("dp", None),
        P("dp"),
        P("dp"),
        P("dp"),
        P("dp"),
        P("dp"),
        P("dp"),
        P("dp"),
        P("dp"),
        P("dp"),
        P(None, "dp"),
        P("dp", None),
    )
    out_specs = (
        P("dp", None),
        P("dp", None),
        P("dp", None),
        P("dp", None),
        P("dp", None),
        P("dp", None),
        P("dp"),
        P("dp"),
        P("dp"),
        P("dp"),
        P("dp"),
        P("dp"),
        P("dp"),
        P("dp"),
        P("dp"),
        P(None, "dp"),
    )
    return jax.shard_map(
        functools.partial(per_device, mesh.shape["dp"]), mesh=mesh, in_specs=in_specs, out_specs=out_specs, check_vma=False
    )
```

```python
import functools
import jax
import jax.numpy as jnp
from jax import lax
from jax.experimental import pallas as pl
from jax.experimental.pallas import tpu as pltpu
from jax.sharding import PartitionSpec as P

HEAD_DIM = 64
PAIR = 2 * HEAD_DIM
EPSILON = 1e-05
SCALE_FACTOR = 0.125
BF16 = jnp.bfloat16
F32 = jnp.float32
NT = (((1,), (1,)), ((), ()))
TN = (((0,), (0,)), ((), ()))


def dot(left, right, dims=(((1,), (0,)), ((), ()))):
    return lax.dot_general(left, right, dims, preferred_element_type=F32)


def normalize(hidden):
    centred = hidden - jnp.mean(hidden, axis=-1, keepdims=True)
    inverse = lax.rsqrt(jnp.mean(centred * centred, axis=-1, keepdims=True) + EPSILON)
    return centred * inverse, inverse


def norm_back(grad_out, gain, normed, inverse):
    scaled = grad_out * gain
    return inverse * (
        scaled
        - jnp.mean(scaled, axis=-1, keepdims=True)
        - normed * jnp.mean(scaled * normed, axis=-1, keepdims=True)
    )


def whole(shape):
    zeros = (0,) * len(shape)
    return pl.BlockSpec(shape, lambda *_: zeros, pipeline_mode=pl.Buffered(1))


def small(megabytes=4):
    return pltpu.CompilerParams(vmem_limit_bytes=megabytes * 1024 * 1024)


def call(kernel, grid, in_specs, out_specs, out_shape, flops, scratch=(), exps=0, name=None, aliases=None, vmem=56):
    moved = sum(s.size * s.dtype.itemsize for s in out_shape) * 2
    return pl.pallas_call(
        kernel,
        grid=grid,
        in_specs=in_specs,
        out_specs=out_specs,
        out_shape=out_shape,
        scratch_shapes=list(scratch),
        input_output_aliases=aliases or {},
        compiler_params=pltpu.CompilerParams(vmem_limit_bytes=vmem * 1024 * 1024),
        cost_estimate=pl.CostEstimate(flops=flops, bytes_accessed=moved, transcendentals=exps),
        name=name,
    )


GAIN_A, SHIFT_A, GAIN_F, SHIFT_F, BIAS_Q, BIAS_V, BIAS_OUT, BIAS_DOWN = range(8)
LANES = 128
TILE = 16


def pack_kernel(w, table, *refs):
    vectors, up, out, held = refs[:8], refs[8], refs[9], refs[10]
    own, steps = table.shape
    cols = w.shape[1]
    held[...] = jnp.zeros_like(held)
    for k, vector in enumerate(vectors):
        held[64 + k : 65 + k, 0:own] = vector[...].astype(F32).reshape(1, own)
    wide = up[...].astype(F32).reshape(1, up.shape[0])
    for k in range(up.shape[0] // own):
        held[72 + k : 73 + k, 0:own] = wide[:, k * own : (k + 1) * own]
    packed = held[...].T[0:own, :].astype(BF16)
    out[:, 0:cols] = w[...]
    out[:, cols:] = packed
    out[:, cols : cols + steps] = table[...]


def pack(w, table, vectors, bias_up):
    own, cols = w.shape
    vmem = pl.BlockSpec(memory_space=pltpu.VMEM)
    return pl.pallas_call(
        pack_kernel,
        in_specs=[vmem] * 11,
        out_specs=vmem,
        out_shape=jax.ShapeDtypeStruct((own, cols + LANES), BF16),
        scratch_shapes=[pltpu.VMEM((LANES, LANES), F32)],
        name="pack",
    )(w, table.T, *vectors, bias_up)


def join_kernel(w_out, w_up, w_down, out):
    own, width = w_out.shape
    edge = width + w_up.shape[1]
    out[:, 0:width] = w_out[...]
    out[:, width:edge] = w_up[...]
    for fold in range(w_down.shape[0] // own):
        out[:, edge + fold * width : edge + (fold + 1) * width] = w_down[fold * own : (fold + 1) * own, :]


def join(w_out, w_up, w_down):
    own, width = w_out.shape
    columns = width + w_up.shape[1] + w_down.shape[0] // own * width
    vmem = pl.BlockSpec(memory_space=pltpu.VMEM)
    return pl.pallas_call(
        join_kernel,
        in_specs=[vmem] * 3,
        out_specs=vmem,
        out_shape=jax.ShapeDtypeStruct((own, columns), BF16),
        name="join",
    )(w_out, w_up, w_down)


def stack_kernel(*refs):
    rows = refs[0].shape[0]
    for k, part in enumerate(refs[:-1]):
        refs[-1][k * rows : (k + 1) * rows, :] = part[...]


def stack(parts):
    rows, cols = parts[0].shape
    vmem = pl.BlockSpec(memory_space=pltpu.VMEM)
    return pl.pallas_call(
        stack_kernel,
        in_specs=[vmem] * len(parts),
        out_specs=vmem,
        out_shape=jax.ShapeDtypeStruct((rows * len(parts), cols), BF16),
        compiler_params=small(),
        name="stack",
    )(*parts)


def folded_place(own, folds, fold, shape, feature_axis):
    feature = lax.broadcasted_iota(jnp.int32, shape, feature_axis)
    unit = lax.broadcasted_iota(jnp.int32, shape, 1 - feature_axis)
    device = lax.div(feature, own)
    place = device * (own * folds) + fold * own + (feature - device * own)
    return jnp.where(unit == place, 1.0, 0.0).astype(BF16)


def split_two(value):
    high = value.astype(BF16)
    return high, (value - high.astype(F32)).astype(BF16)


def rows_at(block, fold=1):
    return pl.ds(pl.multiple_of(block * (TILE * fold), TILE * fold), TILE * fold)


def in_order(me, sources, apart, columns, target):
    for source, steps in zip(sources, apart):
        for block, step in enumerate(steps):
            target[rows_at(me ^ step), :] = source[block * TILE : (block + 1) * TILE, columns]


def project_kernel(apart, own, folds, me_ref, time_ref, tok, *refs):
    sources = refs[: len(apart)]
    proj_out, turned_out, w_out, vec, b_up, tile, held = refs[len(apart) :]
    cols = w_out.shape[1]

    @pl.when(pl.program_id(0) == 0)
    def _():
        me = me_ref[0]
        in_order(me, sources, apart, slice(0, cols), w_out)
        in_order(me, sources, apart, slice(cols, cols + LANES), tile)
        held[...] = tile[...].astype(F32).T
        vec[0:8, :] = held[64:72, :]
        vec[8:9, :] = held[pl.ds(time_ref[0], 1), :]
        vec[9:16, :] = jnp.full((7, vec.shape[1]), time_ref[0].astype(F32))
        wide = jnp.zeros(b_up.shape, F32)
        for fold in range(folds):
            row = held[72 + fold : 73 + fold, :]
            rows = [row[:, at : at + LANES] for at in range(0, row.shape[1], LANES)]
            rows = jnp.concatenate(rows + rows, axis=0)[0:8].astype(BF16)
            wide = wide + dot(rows, folded_place(own, folds, fold, (LANES, LANES * folds), 0))
        b_up[...] = wide

    start = tok[...].astype(F32) + vec[8:9, :]
    normed, _ = normalize(start)
    entry = (normed * vec[GAIN_A : GAIN_A + 1, :] + vec[SHIFT_A : SHIFT_A + 1, :]).astype(BF16)
    turned_out[...] = entry.T
    product = dot(entry, w_out[...])
    width = tok.shape[1]
    proj_out[:, :width] = (product[:, :width] + vec[BIAS_Q : BIAS_Q + 1, :]).astype(BF16)
    proj_out[:, width : 2 * width] = product[:, width : 2 * width].astype(BF16)
    proj_out[:, 2 * width :] = (product[:, 2 * width :] + vec[BIAS_V : BIAS_V + 1, :]).astype(BF16)


def project(me, timesteps, tokens, sources, apart, own, folds, block=512):
    rows, width = tokens.shape
    cols = sources[0].shape[1] - LANES
    smem = pl.BlockSpec(memory_space=pltpu.SMEM)
    return call(
        functools.partial(project_kernel, apart, own, folds),
        (rows // block,),
        [
            smem,
            smem,
            pl.BlockSpec((block, width), lambda i: (i, 0)),
        ]
        + [pl.BlockSpec(memory_space=pltpu.VMEM) for _ in sources],
        [
            pl.BlockSpec((block, cols), lambda i: (i, 0)),
            pl.BlockSpec((width, block), lambda i: (0, i)),
            whole((width, cols)),
            whole((16, width)),
            whole((8, LANES * folds)),
        ],
        [
            jax.ShapeDtypeStruct((rows, cols), BF16),
            jax.ShapeDtypeStruct((width, rows), BF16),
            jax.ShapeDtypeStruct((width, cols), BF16),
            jax.ShapeDtypeStruct((16, width), F32),
            jax.ShapeDtypeStruct((8, LANES * folds), F32),
        ],
        2 * rows * width * cols,
        scratch=[pltpu.VMEM((width, LANES), BF16), pltpu.VMEM((LANES, width), F32)],
        name="project",
        vmem=20,
    )(me, timesteps, tokens, *sources)


def attend_kernel(block, q_ref, k_ref, v_ref, mixed_out, stat_out):
    rows = q_ref.shape[0]
    first = lax.broadcasted_iota(jnp.int32, (1, PAIR), 1) < HEAD_DIM
    keys_in = k_ref[...]
    values = jnp.concatenate([v_ref[...], jnp.ones((rows, PAIR), BF16)], axis=1)
    for at in range(0, rows, block):
        queries = q_ref[at : at + block, :] * BF16(SCALE_FACTOR)
        parts = []
        for head in range(2):
            own = first if head == 0 else jnp.logical_not(first)
            scores = dot(jnp.where(own, queries, BF16(0)), keys_in, NT)
            top = jnp.max(scores, axis=1, keepdims=True)
            raised = jnp.exp(scores - top).astype(BF16)
            both = dot(raised, values)
            total = both[:, PAIR:]
            parts.append((both[:, :PAIR] / total, top + jnp.log(total)))
        mixed_out[at : at + block, :] = jnp.where(first, parts[0][0], parts[1][0]).astype(BF16)
        stat_out[at : at + block, :] = jnp.where(first, parts[1][1], parts[0][1])


def attend(proj, block=256):
    rows, cols = proj.shape
    width = cols // 3
    pairs = width // PAIR
    return call(
        functools.partial(attend_kernel, block),
        (pairs,),
        [
            pl.BlockSpec((rows, PAIR), lambda p: (0, p)),
            pl.BlockSpec((rows, PAIR), lambda p: (0, pairs + p)),
            pl.BlockSpec((rows, PAIR), lambda p: (0, 2 * pairs + p)),
        ],
        [pl.BlockSpec((rows, PAIR), lambda p: (0, p))] * 2,
        [
            jax.ShapeDtypeStruct((rows, width), BF16),
            jax.ShapeDtypeStruct((rows, width), F32),
        ],
        4 * rows * rows * width,
        exps=rows * rows * width // HEAD_DIM,
        name="attend",
        vmem=20,
    )(proj, proj, proj)


def three_parts(value):
    high = value.astype(BF16).astype(F32)
    middle = (value - high).astype(BF16).astype(F32)
    return high, middle, value - high - middle


def attend_back_kernel(
    block, leaving, kept, me_ref, q_ref, k_ref, v_ref, g_ref, mixed_ref, stat_ref, turned_ref, *refs
):
    refs = refs[kept:]
    grad_out, sums_out = refs[:2]
    targets = refs[2 : 2 + len(leaving)]
    held = refs[-1]
    rows = q_ref.shape[0]
    lane = lax.broadcasted_iota(jnp.int32, (1, PAIR), 1)
    first = lane < HEAD_DIM
    spot = lax.rem(lane, HEAD_DIM)
    queries = q_ref[...] * BF16(SCALE_FACTOR)
    grads = g_ref[...]
    product = grads.astype(F32) * mixed_ref[...].astype(F32)
    logs = three_parts(stat_ref[...])
    minus = jnp.where(spot < 3, BF16(-1), BF16(0))

    def beside(own, value, parts):
        extra = jnp.where(
            spot == 0, parts[0], jnp.where(spot == 1, parts[1], jnp.where(spot == 2, parts[2], 0.0))
        )
        return jnp.where(own, value, extra.astype(BF16))

    grad_q = []
    grad_k = []
    grad_v = []
    heads = []
    for head in range(2):
        own = first if head == 0 else jnp.logical_not(first)
        delta = jnp.sum(jnp.where(own, product, 0.0), axis=1, keepdims=True)
        heads.append((own, beside(own, queries, logs), beside(own, grads, three_parts(delta))))
    total_q = [None, None]
    for at in range(0, rows, block):
        keys_in = k_ref[at : at + block, :]
        values = v_ref[at : at + block, :]
        out_k = []
        out_v = []
        for head, (own, queries_wide, grads_wide) in enumerate(heads):
            probs = jnp.exp(dot(jnp.where(own, keys_in, minus), queries_wide, NT))
            out_v.append(dot(probs.astype(BF16), grads))
            spread = dot(jnp.where(own, values, minus), grads_wide, NT)
            inner = (probs * spread).astype(BF16)
            out_k.append(dot(inner, queries))
            part = dot(inner, keys_in, TN)
            total_q[head] = part if total_q[head] is None else total_q[head] + part
        grad_k.append(jnp.where(first, out_k[0], out_k[1]).astype(BF16))
        grad_v.append(jnp.where(first, out_v[0], out_v[1]).astype(BF16))
    grad_q = (jnp.where(first, total_q[0], total_q[1]) * SCALE_FACTOR).astype(BF16)
    joined = jnp.concatenate(
        [grad_q, jnp.concatenate(grad_k, axis=0), jnp.concatenate(grad_v, axis=0)], axis=1
    )
    grad_out[...] = joined
    held[...] = dot(turned_ref[...], joined).astype(BF16)
    me = me_ref[0]
    for target, steps in zip(targets, leaving):
        for place, step in enumerate(steps):
            target[place * TILE : (place + 1) * TILE, :] = held[rows_at(me ^ step), :]
    sums_out[...] = jnp.sum(joined.astype(F32), axis=0, keepdims=True)


def attend_back(me, leaving, proj, grad_mixed, mixed, stats, turned, begin, count, before=(), block=256):
    rows, cols = proj.shape
    width = cols // 3
    pairs = width // PAIR
    column = pl.BlockSpec((rows, PAIR), lambda p: (0, begin + p))
    place = lambda p: (0, begin + p)
    tall = [len(steps) * TILE for steps in leaving]
    inputs = (me, proj, proj, proj, grad_mixed, mixed, stats, turned)
    return call(
        functools.partial(attend_back_kernel, block, leaving, len(before)),
        (count,),
        [
            pl.BlockSpec(memory_space=pltpu.SMEM),
            column,
            pl.BlockSpec((rows, PAIR), lambda p: (0, pairs + begin + p)),
            pl.BlockSpec((rows, PAIR), lambda p: (0, 2 * pairs + begin + p)),
            column,
            column,
            column,
            whole((width, rows)),
        ]
        + [pl.BlockSpec(memory_space=pl.ANY)] * len(before),
        [pl.BlockSpec((rows, 3 * PAIR), place), pl.BlockSpec((1, 3 * PAIR), place)]
        + [pl.BlockSpec((high, 3 * PAIR), place) for high in tall],
        [jax.ShapeDtypeStruct((rows, cols), BF16), jax.ShapeDtypeStruct((1, cols), F32)]
        + [jax.ShapeDtypeStruct((high, cols), BF16) for high in tall],
        count * (10 * rows * rows * PAIR + 6 * rows * width * PAIR),
        scratch=[pltpu.VMEM((width, 3 * PAIR), BF16)],
        exps=2 * count * rows * rows,
        name="attend_back",
        vmem=24,
        aliases={len(inputs) + k: k for k in range(len(before))},
    )(*inputs, *before)


ROOT_HALF = 0.7071067811865476
ROOT_TWO_PI = 0.3989422804014327


def feed_kernel(
    apart,
    leaving,
    me_ref,
    tok,
    mixed,
    cot,
    vec,
    b_up,
    *refs,
):
    sources = refs[: len(apart)]
    refs = refs[len(apart) :]
    output, grad_mid_out, grad_mixed_out = refs[:3]
    targets = refs[3 : 3 + len(leaving)]
    (
        sums_out,
        sums_up_out,
        w_out,
        w_up,
        w_down,
        acc_up,
        acc_out,
        acc_sums,
        acc_sums_up,
        result,
        grad_acc,
    ) = refs[3 + len(leaving) :]
    step = pl.program_id(0)
    bias_out, gain, shift, bias_down = (
        vec[k : k + 1, :] for k in (BIAS_OUT, GAIN_F, SHIFT_F, BIAS_DOWN)
    )
    width = tok.shape[1]
    hidden = w_up.shape[1]
    folds = hidden // width
    edge = width + hidden
    me = me_ref[0]

    @pl.when(step == 0)
    def _():
        in_order(me, sources, apart, slice(0, width), w_out)
        in_order(me, sources, apart, slice(width, edge), w_up)
        for source, steps in zip(sources, apart):
            for block, far in enumerate(steps):
                for fold in range(folds):
                    w_down[rows_at((me ^ far) * folds + fold), :] = source[
                        block * TILE : (block + 1) * TILE,
                        edge + fold * width : edge + (fold + 1) * width,
                    ]

    start = tok[...].astype(F32) + vec[8:9, :]
    middle = start + dot(mixed[...], w_out[...]) + bias_out
    normed, inverse = normalize(middle)
    entry = (normed * gain + shift).astype(BF16)
    entry_t = entry.T
    cot_now = cot[...]
    cot_t = cot_now.T
    chunk = b_up.shape[1]
    result[...] = middle + bias_down
    grad_acc[...] = jnp.zeros_like(middle)
    acc_sums[...] = jnp.zeros_like(acc_sums)
    acc_sums_up[...] = jnp.zeros_like(acc_sums_up)

    @pl.loop(0, hidden // chunk)
    def _(row):
        spot = pl.ds(pl.multiple_of(row * chunk, chunk), chunk)
        up = w_up[:, spot]
        down = w_down[spot, :]
        pre = dot(entry, up) + b_up[pl.ds(row, 1), :]
        cdf = 0.5 + 0.5 * lax.erf(pre * ROOT_HALF)
        act = (pre * cdf).astype(BF16)
        slope = cdf + pre * (ROOT_TWO_PI * jnp.exp(-0.5 * pre * pre))
        result[...] += dot(act, down)
        w_down[spot, :] = dot(cot_t, act).astype(BF16).T
        grad_pre = (dot(cot_now, down, NT) * slope).astype(BF16)
        acc_up[:, spot] = dot(entry_t, grad_pre).astype(BF16)
        acc_sums_up[pl.ds(row, 1), :] = jnp.sum(grad_pre.astype(F32), axis=0, keepdims=True)
        grad_acc[...] += dot(grad_pre, up, NT)

    grad_feed = grad_acc[...]
    output[...] = result[...].astype(BF16)
    grad_res = cot_now.astype(F32)
    grad_mid = grad_res + norm_back(grad_feed, gain, normed, inverse)
    grad_mid_out[...] = grad_mid
    branch = grad_mid.astype(BF16)
    grad_mixed_out[...] = dot(branch, w_out[...], NT).astype(BF16)
    acc_out[...] = dot(mixed[...].T, branch).astype(BF16)
    for k, value in enumerate((grad_feed * normed, grad_feed, branch.astype(F32), grad_res)):
        acc_sums[k : k + 1, :] = jnp.sum(value, axis=0, keepdims=True)

    @pl.when(step == pl.num_programs(0) - 1)
    def _():
        for target, steps in zip(targets, leaving):
            for block, far in enumerate(steps):
                spot = slice(block * TILE, (block + 1) * TILE)
                source = me ^ far
                target[spot, :width] = acc_out[rows_at(source), :]
                target[spot, width:edge] = acc_up[rows_at(source), :]
                for fold in range(folds):
                    target[spot, edge + fold * width : edge + (fold + 1) * width] = w_down[
                        rows_at(source * folds + fold), :
                    ]
        sums_out[...] = acc_sums[...]
        sums_up_out[...] = acc_sums_up[...]


def feed(me, tokens, mixed, cotangent, sources, apart, leaving, vec, b_up):
    rows, width = tokens.shape
    block = rows
    columns = sources[0].shape[1]
    hidden = (columns - width) // 2
    blocked = pl.BlockSpec((block, width), lambda i: (i, 0))
    return call(
        functools.partial(feed_kernel, apart, leaving),
        (rows // block,),
        [
            pl.BlockSpec(memory_space=pltpu.SMEM),
            blocked,
            blocked,
            blocked,
            whole(vec.shape),
            whole(b_up.shape),
        ]
        + [pl.BlockSpec(memory_space=pltpu.VMEM) for _ in sources],
        [
            blocked,
            blocked,
            blocked,
        ]
        + [pl.BlockSpec(memory_space=pltpu.VMEM) for _ in leaving]
        + [
            whole((8, width)),
            whole(b_up.shape),
        ],
        [
            jax.ShapeDtypeStruct((rows, width), BF16),
            jax.ShapeDtypeStruct((rows, width), F32),
            jax.ShapeDtypeStruct((rows, width), BF16),
        ]
        + [jax.ShapeDtypeStruct((len(steps) * TILE, columns), BF16) for steps in leaving]
        + [
            jax.ShapeDtypeStruct((8, width), F32),
            jax.ShapeDtypeStruct(b_up.shape, F32),
        ],
        12 * rows * width * hidden + 6 * rows * width * width,
        scratch=[
            pltpu.VMEM((width, width), BF16),
            pltpu.VMEM((width, hidden), BF16),
            pltpu.VMEM((hidden, width), BF16),
            pltpu.VMEM((width, hidden), BF16),
            pltpu.VMEM((width, width), BF16),
            pltpu.VMEM((8, width), F32),
            pltpu.VMEM(b_up.shape, F32),
            pltpu.VMEM((rows, width), F32),
            pltpu.VMEM((rows, width), F32),
        ],
        exps=2 * rows * hidden,
        name="feed",
        vmem=46,
    )(me, tokens, mixed, cotangent, vec, b_up, *sources)


def finish_kernel(own, tok, vec, grad_mid, w, feed_sums, up_sums, proj_sums, grad_proj, grad_out, sums_out, acc):
    step = pl.program_id(0)
    normed, inverse = normalize(tok[...].astype(F32) + vec[8:9, :])
    width = tok.shape[1]
    pairs = width // PAIR
    folds = up_sums.shape[1] // LANES
    columns = [w[:, (kind * pairs + k) * PAIR : (kind * pairs + k + 1) * PAIR] for k in range(pairs) for kind in range(3)]
    grad_attn = dot(grad_proj[...], jnp.concatenate(columns, axis=1), NT)
    gain = vec[GAIN_A : GAIN_A + 1, :]
    grad_start = grad_mid[...] + norm_back(grad_attn, gain, normed, inverse)
    grad_out[...] = grad_start

    @pl.when(step == 0)
    def _():
        acc[...] = jnp.zeros_like(acc)

    for k, value in enumerate((grad_start, grad_attn * normed, grad_attn)):
        acc[k : k + 1, :] += jnp.sum(value, axis=0, keepdims=True)

    @pl.when(step == pl.num_programs(0) - 1)
    def _():
        acc[3:7, :] = feed_sums[0:4, :]
        up_high, up_low = split_two(up_sums[...])
        for fold in range(folds):
            place = folded_place(own, folds, fold, (LANES * folds, LANES), 1)
            rows = dot(up_high, place) + dot(up_low, place)
            for k in range(width // LANES):
                acc[7 + fold : 8 + fold, k * LANES : (k + 1) * LANES] = rows[k : k + 1, :]
        for k in range(pairs):
            acc[11:12, k * PAIR : (k + 1) * PAIR] = proj_sums[:, 3 * k * PAIR : (3 * k + 1) * PAIR]
            acc[12:13, k * PAIR : (k + 1) * PAIR] = proj_sums[
                :, (3 * k + 2) * PAIR : (3 * k + 3) * PAIR
            ]
        acc[TIME : TIME + 1, :] = vec[9:10, :]
        high, low = split_two(acc[...].T)
        half = acc.shape[0] // 2
        lane = lax.broadcasted_iota(jnp.int32, (1, acc.shape[0]), 1)
        shifted = pltpu.roll(low.astype(F32), half, 1)
        sums_out[...] = jnp.where(lane < half, high.astype(F32), shifted).astype(BF16)


TIME = 13


def finish(own, tokens, vec, grad_mid, w, feed_sums, up_sums, proj_sums, grad_proj, block=512):
    rows, width = tokens.shape
    blocked = pl.BlockSpec((block, width), lambda i: (i, 0))
    return call(
        functools.partial(finish_kernel, own),
        (rows // block,),
        [
            blocked,
            whole(vec.shape),
            blocked,
            whole(w.shape),
            whole(feed_sums.shape),
            whole(up_sums.shape),
            whole(proj_sums.shape),
            pl.BlockSpec((block, grad_proj.shape[1]), lambda i: (i, 0)),
        ],
        [blocked, whole((width, LANES))],
        [
            jax.ShapeDtypeStruct((rows, width), F32),
            jax.ShapeDtypeStruct((width, LANES), BF16),
        ],
        6 * rows * width * width,
        scratch=[pltpu.VMEM((LANES, width), F32)],
        name="finish",
        vmem=20,
    )(tokens, vec, grad_mid, w, feed_sums, up_sums, proj_sums, grad_proj)


SUM_ROWS = (1, 2, 3, 4, 11, 12, 5, 6)


def collect_kernel(folds, parts, *refs):
    vectors, up, table_out, held = refs[:-3], refs[-3], refs[-2], refs[-1]
    count, own, _ = parts.shape
    lane = lax.broadcasted_iota(jnp.int32, (1, LANES), 1).astype(F32)
    total = jnp.zeros((own, LANES), F32)
    table = jnp.zeros((own, LANES), F32)
    for source in range(count):
        part = parts[source].astype(F32)
        part = part + pltpu.roll(part, LANES // 2, 1)
        total = total + part
        table = table + jnp.where(lane == part[:, TIME : TIME + 1], part[:, 0:1], 0.0)
    held[...] = jnp.zeros_like(held)
    held[0:own, :] = total
    turned = held[...].T
    for k, out in zip(SUM_ROWS, vectors):
        out[...] = turned[k, 0:own]
    wide = turned[7:8, :]
    for fold in range(1, folds):
        wide = wide + pltpu.roll(turned[7 + fold : 8 + fold, :], fold * own, 1)
    up[...] = wide[0, 0 : folds * own]
    table_out[...] = table[:, 0 : table_out.shape[1]]


def collect(parts, steps, folds):
    own = parts.shape[1]
    vmem = pl.BlockSpec(memory_space=pltpu.VMEM)
    return pl.pallas_call(
        functools.partial(collect_kernel, folds),
        in_specs=[vmem],
        out_specs=[vmem] * 10,
        out_shape=[jax.ShapeDtypeStruct((own,), F32)] * 8
        + [jax.ShapeDtypeStruct((own * folds,), F32), jax.ShapeDtypeStruct((own, steps), F32)],
        scratch_shapes=[pltpu.VMEM((LANES, LANES), F32)],
        compiler_params=small(),
        name="collect",
    )(parts)


def settle_kernel(count, *refs):
    parts, outs = refs[:count], refs[count:]
    value = parts[0][...].astype(F32)
    for part in parts[1:]:
        value = value + part[...].astype(F32)
    own = value.shape[0]
    if len(outs) == 1:
        pairs = value.shape[1] // (3 * PAIR)
        for pair in range(pairs):
            for kind in range(3):
                at = (3 * pair + kind) * PAIR
                spot = (kind * pairs + pair) * PAIR
                outs[0][:, spot : spot + PAIR] = value[:, at : at + PAIR]
    else:
        w_out, w_up, w_down = outs
        width = w_out.shape[1]
        edge = width + w_up.shape[1]
        w_out[...] = value[:, :width]
        w_up[...] = value[:, width:edge]
        for fold in range(w_down.shape[0] // own):
            w_down[fold * own : (fold + 1) * own, :] = value[:, edge + fold * width : edge + (fold + 1) * width]


def settle(parts, shapes, name):
    vmem = pl.BlockSpec(memory_space=pltpu.VMEM)
    return pl.pallas_call(
        functools.partial(settle_kernel, len(parts)),
        in_specs=[vmem] * len(parts),
        out_specs=[vmem] * len(shapes),
        out_shape=[jax.ShapeDtypeStruct(shape, F32) for shape in shapes],
        compiler_params=small(),
        name=name,
    )(*parts)


def levels_of(count):
    bits = (count - 1).bit_length()
    if count != 1 << bits:
        raise ValueError("device count")
    return [[0]] + [list(range(at, min(at + 2, bits))) for at in range(1, bits, 2)]


def masks_of(bits):
    return [step << bits[0] for step in range(1 << len(bits))]


def permute(value, mask, count):
    return lax.ppermute(value, "dp", [(device, device ^ mask) for device in range(count)])


def gather_level(value, bits, count):
    return [value] + [permute(value, mask, count) for mask in masks_of(bits)[1:]]


def total(parts):
    result = parts[0].astype(F32)
    for part in parts[1:]:
        result = result + part.astype(F32)
    return result


def reduce_level(pieces, bits, count):
    return [pieces[0]] + [
        permute(piece, mask, count) for piece, mask in zip(pieces[1:], masks_of(bits)[1:])
    ]


def fold_down(rows, folds, own, back):
    width = rows.shape[1] // folds
    old, new = (TILE, own) if back else (own, TILE)
    rows = rows.reshape(-1, old, folds, width).transpose(0, 2, 1, 3)
    rows = rows.reshape(-1, folds, new, width).transpose(0, 2, 1, 3)
    return rows.reshape(-1, folds * width)


def refold(value, folded, folds, own, back):
    if not folded:
        return value
    edge = value.shape[1] - folded
    return jnp.concatenate([value[:, :edge], fold_down(value[:, edge:], folds, own, back)], axis=1)


class Plan:
    def __init__(self, count, own, folds):
        self.count, self.own, self.folds = count, own, folds
        self.levels = levels_of(count)
        self.tiled = own == TILE and len(self.levels) == 3
        index = lax.axis_index("dp").astype(jnp.int32)
        if self.tiled:
            near, middle, far = (masks_of(bits) for bits in self.levels)
            self.apart = tuple(
                tuple(a + b + c for c in far) for a in near for b in middle
            )
            self.leaving = tuple(tuple(a + b + c for b in middle for c in far) for a in near)
            self.me = index.reshape(1)
        else:
            self.index = index
            self.apart = self.leaving = (tuple(range(own * count // TILE)),)
            self.me = jnp.zeros((1,), jnp.int32)

    def spread(self, shard, level):
        return gather_level(shard, self.levels[level], self.count)

    def near(self, halves):
        keep, send = halves
        return keep, permute(send, 1, self.count)

    def cut(self, parts):
        size = parts[0].shape[0] // 4
        return [
            total([part[k * size : (k + 1) * size] for part in parts]).astype(BF16)
            for k in range(4)
        ]

    def around(self, pieces):
        return reduce_level(pieces, self.levels[1], self.count)

    def far(self, pieces):
        return reduce_level(pieces, self.levels[2], self.count)

    def whole(self, shard, folded):
        value = shard
        for bits in reversed(self.levels):
            value = jnp.stack(gather_level(value, bits, self.count))
        value = value.reshape((self.count,) + shard.shape)
        value = value[self.places() ^ self.place(self.index)]
        return refold(value.reshape(-1, shard.shape[1]), folded, self.folds, self.own, False)

    def place(self, device):
        result = 0
        for bits in self.levels:
            result = (result << len(bits)) | ((device >> bits[0]) & ((1 << len(bits)) - 1))
        return result

    def places(self):
        return self.place(jnp.arange(self.count, dtype=jnp.int32))

    def sum_whole(self, value, folded):
        value = refold(value, folded, self.folds, self.own, True)
        value = value.reshape(self.count, self.own, -1)
        order = [0] * self.count
        for device in range(self.count):
            order[self.place(device)] = device
        value = value[jnp.array(order, jnp.int32) ^ self.index]
        for at, bits in enumerate(self.levels):
            value = value.reshape((1 << len(bits), -1) + value.shape[1:])
            value = total(reduce_level(list(value), bits, self.count))
            if at < len(self.levels) - 1:
                value = value.astype(BF16)
        return value.reshape(self.own, -1)


def after(value, *done):
    leaves, tree = jax.tree.flatten(value)
    return jax.tree.unflatten(tree, lax.optimization_barrier((*leaves, *done))[: len(leaves)])


def exchange(value):
    return lax.all_to_all(value, "dp", 0, 0, tiled=True)


def per_device(
    count,
    tokens,
    timesteps,
    w_qkv,
    w_out,
    w_up,
    w_down,
    gain_attn,
    shift_attn,
    gain_ffn,
    shift_ffn,
    bias_query,
    bias_value,
    bias_out,
    bias_up,
    bias_down,
    step_table,
    cotangent,
):
    rows, width = tokens.shape
    own = width // count
    steps = step_table.shape[0]
    hidden = w_up.shape[1]
    folds = hidden // width
    edge = width + hidden
    plan = Plan(count, own, folds)
    pairs = width // PAIR

    vectors = (
        gain_attn,
        shift_attn,
        gain_ffn,
        shift_ffn,
        bias_query,
        bias_value,
        bias_out,
        bias_down,
    )
    plan.me = after(plan.me, w_qkv)
    w_qkv = after(w_qkv, plan.me)
    entry = pack(w_qkv, step_table, vectors, bias_up)
    if plan.tiled:
        joint = join(w_out, w_up, w_down)
        far = plan.spread(entry, 2)
        joint = plan.spread(joint, 2)
        entry = jnp.concatenate(far, axis=0)
        entries = plan.spread(entry, 1)
        joint = jnp.concatenate(after(joint, *entries[1:]), axis=0)
        entries = entries + [permute(entry, 1, count) for entry in entries]
        joints = plan.spread(joint, 1)
    else:
        joint = jnp.concatenate(
            [w_out, w_up] + [w_down[k * own : (k + 1) * own] for k in range(folds)], axis=1
        )
        entries = [plan.whole(entry, 0)]
        joints = [plan.whole(joint, hidden)]

    proj, turned, full_qkv, vec, up_bias = project(
        plan.me, timesteps, tokens, entries, plan.apart, own, folds
    )
    mixed, stats = attend(proj)

    if plan.tiled:
        joints[1:] = after(joints[1:], mixed)
        joints = joints + [permute(joint, 1, count) for joint in joints]
    feed_out = feed(
        plan.me, tokens, mixed, cotangent, joints, plan.apart, plan.leaving, vec, up_bias
    )
    output, grad_mid, grad_mixed = feed_out[:3]
    feed_sums, up_sums = feed_out[-2:]

    def back(grad_mixed, begin, number, before=()):
        return attend_back(
            plan.me, plan.leaving, proj, grad_mixed, mixed, stats, turned, begin, number, before
        )

    if plan.tiled:
        near = plan.near(feed_out[3:5])
        first = back(grad_mixed, 0, 1)
        pieces = plan.cut(after(near, first[0]))
        grad_proj, proj_sums, *leaving = back(after(grad_mixed, *pieces), 1, pairs - 1, first)
        pieces = plan.cut(after(plan.around(pieces), grad_proj))
        near = plan.near(leaving)
        grad_mid = after(grad_mid, *pieces)
    else:
        grad_proj, proj_sums, leaving = back(grad_mixed, 0, pairs)
        sum_parts = [plan.sum_whole(feed_out[3], hidden)]
        weight_parts = [plan.sum_whole(leaving, 0)]

    grad_start, packed_sums = finish(
        own, tokens, vec, grad_mid, full_qkv, feed_sums, up_sums, proj_sums, grad_proj
    )
    parts = exchange(packed_sums.reshape(count, own, LANES))
    if plan.tiled:
        sum_parts = plan.far(pieces)
        pieces = plan.around(plan.cut(after(near, grad_start)))
        weight_parts = plan.far(plan.cut(pieces))
    *sums, sum_up, sum_table = collect(parts, steps, folds)
    sum_out, sum_w_up, sum_down = settle(
        sum_parts, (w_out.shape, w_up.shape, w_down.shape), "settle_joint"
    )
    (sum_qkv,) = settle(weight_parts, (w_qkv.shape,), "settle_qkv")
    return (
        output,
        grad_start,
        sum_qkv,
        sum_out,
        sum_w_up,
        sum_down,
        *sums[:7],
        sum_up,
        sums[7],
        sum_table.T,
    )


def solution(mesh):
    in_specs = (
        P("dp", None),
        P("dp"),
        P("dp", None),
        P("dp", None),
        P("dp", None),
        P("dp", None),
        P("dp"),
        P("dp"),
        P("dp"),
        P("dp"),
        P("dp"),
        P("dp"),
        P("dp"),
        P("dp"),
        P("dp"),
        P(None, "dp"),
        P("dp", None),
    )
    out_specs = (
        P("dp", None),
        P("dp", None),
        P("dp", None),
        P("dp", None),
        P("dp", None),
        P("dp", None),
        P("dp"),
        P("dp"),
        P("dp"),
        P("dp"),
        P("dp"),
        P("dp"),
        P("dp"),
        P("dp"),
        P("dp"),
        P(None, "dp"),
    )
    return jax.shard_map(
        functools.partial(per_device, mesh.shape["dp"]), mesh=mesh, in_specs=in_specs, out_specs=out_specs, check_vma=False
    )
```

```python
import functools
import jax
import jax.numpy as jnp
from jax import lax
from jax.experimental import pallas as pl
from jax.experimental.pallas import tpu as pltpu
from jax.sharding import PartitionSpec as P

HEAD_DIM = 64
PAIR = 2 * HEAD_DIM
EPSILON = 1e-05
SCALE_FACTOR = 0.125
BF16 = jnp.bfloat16
F32 = jnp.float32
NT = (((1,), (1,)), ((), ()))
TN = (((0,), (0,)), ((), ()))


def dot(left, right, dims=(((1,), (0,)), ((), ()))):
    return lax.dot_general(left, right, dims, preferred_element_type=F32)


def normalize(hidden):
    centred = hidden - jnp.mean(hidden, axis=-1, keepdims=True)
    inverse = lax.rsqrt(jnp.mean(centred * centred, axis=-1, keepdims=True) + EPSILON)
    return centred * inverse, inverse


def norm_back(grad_out, gain, normed, inverse):
    scaled = grad_out * gain
    return inverse * (
        scaled
        - jnp.mean(scaled, axis=-1, keepdims=True)
        - normed * jnp.mean(scaled * normed, axis=-1, keepdims=True)
    )


def whole(shape):
    zeros = (0,) * len(shape)
    return pl.BlockSpec(shape, lambda *_: zeros, pipeline_mode=pl.Buffered(1))


def small(megabytes=4):
    return pltpu.CompilerParams(vmem_limit_bytes=megabytes * 1024 * 1024)


def call(kernel, grid, in_specs, out_specs, out_shape, flops, scratch=(), exps=0, name=None, aliases=None, vmem=56):
    moved = sum(s.size * s.dtype.itemsize for s in out_shape) * 2
    return pl.pallas_call(
        kernel,
        grid=grid,
        in_specs=in_specs,
        out_specs=out_specs,
        out_shape=out_shape,
        scratch_shapes=list(scratch),
        input_output_aliases=aliases or {},
        compiler_params=pltpu.CompilerParams(vmem_limit_bytes=vmem * 1024 * 1024),
        cost_estimate=pl.CostEstimate(flops=flops, bytes_accessed=moved, transcendentals=exps),
        name=name,
    )


GAIN_A, SHIFT_A, GAIN_F, SHIFT_F, BIAS_Q, BIAS_V, BIAS_OUT, BIAS_DOWN = range(8)
LANES = 128
TILE = 16


def pack_kernel(w, table, *refs):
    vectors, up, out, held = refs[:8], refs[8], refs[9], refs[10]
    own, steps = table.shape
    cols = w.shape[1]
    held[...] = jnp.zeros_like(held)
    for k, vector in enumerate(vectors):
        held[64 + k : 65 + k, 0:own] = vector[...].astype(F32).reshape(1, own)
    wide = up[...].astype(F32).reshape(1, up.shape[0])
    for k in range(up.shape[0] // own):
        held[72 + k : 73 + k, 0:own] = wide[:, k * own : (k + 1) * own]
    packed = held[...].T[0:own, :].astype(BF16)
    out[:, 0:cols] = w[...]
    out[:, cols:] = packed
    out[:, cols : cols + steps] = table[...]


def pack(w, table, vectors, bias_up):
    own, cols = w.shape
    vmem = pl.BlockSpec(memory_space=pltpu.VMEM)
    return pl.pallas_call(
        pack_kernel,
        in_specs=[vmem] * 11,
        out_specs=vmem,
        out_shape=jax.ShapeDtypeStruct((own, cols + LANES), BF16),
        scratch_shapes=[pltpu.VMEM((LANES, LANES), F32)],
        name="pack",
    )(w, table.T, *vectors, bias_up)


def join_kernel(w_out, w_up, w_down, out):
    own, width = w_out.shape
    edge = width + w_up.shape[1]
    out[:, 0:width] = w_out[...]
    out[:, width:edge] = w_up[...]
    for fold in range(w_down.shape[0] // own):
        out[:, edge + fold * width : edge + (fold + 1) * width] = w_down[fold * own : (fold + 1) * own, :]


def join(w_out, w_up, w_down):
    own, width = w_out.shape
    columns = width + w_up.shape[1] + w_down.shape[0] // own * width
    vmem = pl.BlockSpec(memory_space=pltpu.VMEM)
    return pl.pallas_call(
        join_kernel,
        in_specs=[vmem] * 3,
        out_specs=vmem,
        out_shape=jax.ShapeDtypeStruct((own, columns), BF16),
        name="join",
    )(w_out, w_up, w_down)


def stack_kernel(*refs):
    rows = refs[0].shape[0]
    for k, part in enumerate(refs[:-1]):
        refs[-1][k * rows : (k + 1) * rows, :] = part[...]


def stack(parts):
    rows, cols = parts[0].shape
    vmem = pl.BlockSpec(memory_space=pltpu.VMEM)
    return pl.pallas_call(
        stack_kernel,
        in_specs=[vmem] * len(parts),
        out_specs=vmem,
        out_shape=jax.ShapeDtypeStruct((rows * len(parts), cols), BF16),
        compiler_params=small(),
        name="stack",
    )(*parts)


def folded_place(own, folds, fold, shape, feature_axis):
    feature = lax.broadcasted_iota(jnp.int32, shape, feature_axis)
    unit = lax.broadcasted_iota(jnp.int32, shape, 1 - feature_axis)
    device = lax.div(feature, own)
    place = device * (own * folds) + fold * own + (feature - device * own)
    return jnp.where(unit == place, 1.0, 0.0).astype(BF16)


def split_two(value):
    high = value.astype(BF16)
    return high, (value - high.astype(F32)).astype(BF16)


def rows_at(block, fold=1):
    return pl.ds(pl.multiple_of(block * (TILE * fold), TILE * fold), TILE * fold)


def in_order(me, sources, apart, columns, target):
    for source, steps in zip(sources, apart):
        for block, step in enumerate(steps):
            target[rows_at(me ^ step), :] = source[block * TILE : (block + 1) * TILE, columns]


def project_kernel(apart, own, folds, me_ref, time_ref, tok, *refs):
    sources = refs[: len(apart)]
    proj_out, turned_out, w_out, vec, b_up, tile, held = refs[len(apart) :]
    cols = w_out.shape[1]

    @pl.when(pl.program_id(0) == 0)
    def _():
        me = me_ref[0]
        in_order(me, sources, apart, slice(0, cols), w_out)
        in_order(me, sources, apart, slice(cols, cols + LANES), tile)
        held[...] = tile[...].astype(F32).T
        vec[0:8, :] = held[64:72, :]
        vec[8:9, :] = held[pl.ds(time_ref[0], 1), :]
        vec[9:16, :] = jnp.full((7, vec.shape[1]), time_ref[0].astype(F32))
        wide = jnp.zeros(b_up.shape, F32)
        for fold in range(folds):
            row = held[72 + fold : 73 + fold, :]
            rows = [row[:, at : at + LANES] for at in range(0, row.shape[1], LANES)]
            rows = jnp.concatenate(rows + rows, axis=0)[0:8].astype(BF16)
            wide = wide + dot(rows, folded_place(own, folds, fold, (LANES, LANES * folds), 0))
        b_up[...] = wide

    start = tok[...].astype(F32) + vec[8:9, :]
    normed, _ = normalize(start)
    entry = (normed * vec[GAIN_A : GAIN_A + 1, :] + vec[SHIFT_A : SHIFT_A + 1, :]).astype(BF16)
    turned_out[...] = entry.T
    product = dot(entry, w_out[...])
    width = tok.shape[1]
    proj_out[:, :width] = (product[:, :width] + vec[BIAS_Q : BIAS_Q + 1, :]).astype(BF16)
    proj_out[:, width : 2 * width] = product[:, width : 2 * width].astype(BF16)
    proj_out[:, 2 * width :] = (product[:, 2 * width :] + vec[BIAS_V : BIAS_V + 1, :]).astype(BF16)


def project(me, timesteps, tokens, sources, apart, own, folds, block=512):
    rows, width = tokens.shape
    cols = sources[0].shape[1] - LANES
    smem = pl.BlockSpec(memory_space=pltpu.SMEM)
    return call(
        functools.partial(project_kernel, apart, own, folds),
        (rows // block,),
        [
            smem,
            smem,
            pl.BlockSpec((block, width), lambda i: (i, 0)),
        ]
        + [pl.BlockSpec(memory_space=pltpu.VMEM) for _ in sources],
        [
            pl.BlockSpec((block, cols), lambda i: (i, 0)),
            pl.BlockSpec((width, block), lambda i: (0, i)),
            whole((width, cols)),
            whole((16, width)),
            whole((8, LANES * folds)),
        ],
        [
            jax.ShapeDtypeStruct((rows, cols), BF16),
            jax.ShapeDtypeStruct((width, rows), BF16),
            jax.ShapeDtypeStruct((width, cols), BF16),
            jax.ShapeDtypeStruct((16, width), F32),
            jax.ShapeDtypeStruct((8, LANES * folds), F32),
        ],
        2 * rows * width * cols,
        scratch=[pltpu.VMEM((width, LANES), BF16), pltpu.VMEM((LANES, width), F32)],
        name="project",
        vmem=20,
    )(me, timesteps, tokens, *sources)


def attend_kernel(block, q_ref, k_ref, v_ref, mixed_out, stat_out):
    rows = q_ref.shape[0]
    first = lax.broadcasted_iota(jnp.int32, (1, PAIR), 1) < HEAD_DIM
    keys_in = k_ref[...]
    values = jnp.concatenate([v_ref[...], jnp.ones((rows, PAIR), BF16)], axis=1)
    for at in range(0, rows, block):
        queries = q_ref[at : at + block, :] * BF16(SCALE_FACTOR)
        parts = []
        for head in range(2):
            own = first if head == 0 else jnp.logical_not(first)
            scores = dot(jnp.where(own, queries, BF16(0)), keys_in, NT)
            top = jnp.max(scores, axis=1, keepdims=True)
            raised = jnp.exp(scores - top).astype(BF16)
            both = dot(raised, values)
            total = both[:, PAIR:]
            parts.append((both[:, :PAIR] / total, top + jnp.log(total)))
        mixed_out[at : at + block, :] = jnp.where(first, parts[0][0], parts[1][0]).astype(BF16)
        stat_out[at : at + block, :] = jnp.where(first, parts[1][1], parts[0][1])


def attend(proj, block=256):
    rows, cols = proj.shape
    width = cols // 3
    pairs = width // PAIR
    return call(
        functools.partial(attend_kernel, block),
        (pairs,),
        [
            pl.BlockSpec((rows, PAIR), lambda p: (0, p)),
            pl.BlockSpec((rows, PAIR), lambda p: (0, pairs + p)),
            pl.BlockSpec((rows, PAIR), lambda p: (0, 2 * pairs + p)),
        ],
        [pl.BlockSpec((rows, PAIR), lambda p: (0, p))] * 2,
        [
            jax.ShapeDtypeStruct((rows, width), BF16),
            jax.ShapeDtypeStruct((rows, width), F32),
        ],
        4 * rows * rows * width,
        exps=rows * rows * width // HEAD_DIM,
        name="attend",
        vmem=20,
    )(proj, proj, proj)


def three_parts(value):
    high = value.astype(BF16).astype(F32)
    middle = (value - high).astype(BF16).astype(F32)
    return high, middle, value - high - middle


def attend_back_kernel(
    block, leaving, kept, me_ref, q_ref, k_ref, v_ref, g_ref, mixed_ref, stat_ref, turned_ref, *refs
):
    refs = refs[kept:]
    grad_out, sums_out = refs[:2]
    targets = refs[2 : 2 + len(leaving)]
    held = refs[-1]
    rows = q_ref.shape[0]
    lane = lax.broadcasted_iota(jnp.int32, (1, PAIR), 1)
    first = lane < HEAD_DIM
    spot = lax.rem(lane, HEAD_DIM)
    queries = q_ref[...] * BF16(SCALE_FACTOR)
    grads = g_ref[...]
    product = grads.astype(F32) * mixed_ref[...].astype(F32)
    logs = three_parts(stat_ref[...])
    minus = jnp.where(spot < 3, BF16(-1), BF16(0))

    def beside(own, value, parts):
        extra = jnp.where(
            spot == 0, parts[0], jnp.where(spot == 1, parts[1], jnp.where(spot == 2, parts[2], 0.0))
        )
        return jnp.where(own, value, extra.astype(BF16))

    grad_q = []
    grad_k = []
    grad_v = []
    heads = []
    for head in range(2):
        own = first if head == 0 else jnp.logical_not(first)
        delta = jnp.sum(jnp.where(own, product, 0.0), axis=1, keepdims=True)
        heads.append((own, beside(own, queries, logs), beside(own, grads, three_parts(delta))))
    total_q = [None, None]
    for at in range(0, rows, block):
        keys_in = k_ref[at : at + block, :]
        values = v_ref[at : at + block, :]
        out_k = []
        out_v = []
        for head, (own, queries_wide, grads_wide) in enumerate(heads):
            probs = jnp.exp(dot(jnp.where(own, keys_in, minus), queries_wide, NT))
            out_v.append(dot(probs.astype(BF16), grads))
            spread = dot(jnp.where(own, values, minus), grads_wide, NT)
            inner = (probs * spread).astype(BF16)
            out_k.append(dot(inner, queries))
            part = dot(inner, keys_in, TN)
            total_q[head] = part if total_q[head] is None else total_q[head] + part
        grad_k.append(jnp.where(first, out_k[0], out_k[1]).astype(BF16))
        grad_v.append(jnp.where(first, out_v[0], out_v[1]).astype(BF16))
    grad_q = (jnp.where(first, total_q[0], total_q[1]) * SCALE_FACTOR).astype(BF16)
    joined = jnp.concatenate(
        [grad_q, jnp.concatenate(grad_k, axis=0), jnp.concatenate(grad_v, axis=0)], axis=1
    )
    grad_out[...] = joined
    held[...] = dot(turned_ref[...], joined).astype(BF16)
    me = me_ref[0]
    for target, steps in zip(targets, leaving):
        for place, step in enumerate(steps):
            target[place * TILE : (place + 1) * TILE, :] = held[rows_at(me ^ step), :]
    sums_out[...] = jnp.sum(joined.astype(F32), axis=0, keepdims=True)


def attend_back(me, leaving, proj, grad_mixed, mixed, stats, turned, begin, count, before=(), block=256):
    rows, cols = proj.shape
    width = cols // 3
    pairs = width // PAIR
    column = pl.BlockSpec((rows, PAIR), lambda p: (0, begin + p))
    place = lambda p: (0, begin + p)
    tall = [len(steps) * TILE for steps in leaving]
    inputs = (me, proj, proj, proj, grad_mixed, mixed, stats, turned)
    return call(
        functools.partial(attend_back_kernel, block, leaving, len(before)),
        (count,),
        [
            pl.BlockSpec(memory_space=pltpu.SMEM),
            column,
            pl.BlockSpec((rows, PAIR), lambda p: (0, pairs + begin + p)),
            pl.BlockSpec((rows, PAIR), lambda p: (0, 2 * pairs + begin + p)),
            column,
            column,
            column,
            whole((width, rows)),
        ]
        + [pl.BlockSpec(memory_space=pl.ANY)] * len(before),
        [pl.BlockSpec((rows, 3 * PAIR), place), pl.BlockSpec((1, 3 * PAIR), place)]
        + [pl.BlockSpec((high, 3 * PAIR), place) for high in tall],
        [jax.ShapeDtypeStruct((rows, cols), BF16), jax.ShapeDtypeStruct((1, cols), F32)]
        + [jax.ShapeDtypeStruct((high, cols), BF16) for high in tall],
        count * (10 * rows * rows * PAIR + 6 * rows * width * PAIR),
        scratch=[pltpu.VMEM((width, 3 * PAIR), BF16)],
        exps=2 * count * rows * rows,
        name="attend_back",
        vmem=24,
        aliases={len(inputs) + k: k for k in range(len(before))},
    )(*inputs, *before)


ROOT_HALF = 0.7071067811865476
ROOT_TWO_PI = 0.3989422804014327


def feed_kernel(
    apart,
    leaving,
    me_ref,
    tok,
    mixed,
    cot,
    vec,
    b_up,
    *refs,
):
    sources = refs[: len(apart)]
    refs = refs[len(apart) :]
    output, grad_mid_out, grad_mixed_out = refs[:3]
    targets = refs[3 : 3 + len(leaving)]
    (
        sums_out,
        sums_up_out,
        w_out,
        w_up,
        w_down,
        acc_up,
        acc_out,
        acc_sums,
        acc_sums_up,
        result,
        grad_acc,
    ) = refs[3 + len(leaving) :]
    step = pl.program_id(0)
    bias_out, gain, shift, bias_down = (
        vec[k : k + 1, :] for k in (BIAS_OUT, GAIN_F, SHIFT_F, BIAS_DOWN)
    )
    width = tok.shape[1]
    hidden = w_up.shape[1]
    folds = hidden // width
    edge = width + hidden
    me = me_ref[0]

    @pl.when(step == 0)
    def _():
        in_order(me, sources, apart, slice(0, width), w_out)
        in_order(me, sources, apart, slice(width, edge), w_up)
        for source, steps in zip(sources, apart):
            for block, far in enumerate(steps):
                for fold in range(folds):
                    w_down[rows_at((me ^ far) * folds + fold), :] = source[
                        block * TILE : (block + 1) * TILE,
                        edge + fold * width : edge + (fold + 1) * width,
                    ]

    start = tok[...].astype(F32) + vec[8:9, :]
    middle = start + dot(mixed[...], w_out[...]) + bias_out
    normed, inverse = normalize(middle)
    entry = (normed * gain + shift).astype(BF16)
    entry_t = entry.T
    cot_now = cot[...]
    cot_t = cot_now.T
    chunk = b_up.shape[1]
    result[...] = middle + bias_down
    grad_acc[...] = jnp.zeros_like(middle)
    acc_sums[...] = jnp.zeros_like(acc_sums)
    acc_sums_up[...] = jnp.zeros_like(acc_sums_up)

    @pl.loop(0, hidden // chunk)
    def _(row):
        spot = pl.ds(pl.multiple_of(row * chunk, chunk), chunk)
        up = w_up[:, spot]
        down = w_down[spot, :]
        pre = dot(entry, up) + b_up[pl.ds(row, 1), :]
        cdf = 0.5 + 0.5 * lax.erf(pre * ROOT_HALF)
        act = (pre * cdf).astype(BF16)
        slope = cdf + pre * (ROOT_TWO_PI * jnp.exp(-0.5 * pre * pre))
        result[...] += dot(act, down)
        w_down[spot, :] = dot(cot_t, act).astype(BF16).T
        grad_pre = (dot(cot_now, down, NT) * slope).astype(BF16)
        acc_up[:, spot] = dot(entry_t, grad_pre).astype(BF16)
        acc_sums_up[pl.ds(row, 1), :] = jnp.sum(grad_pre.astype(F32), axis=0, keepdims=True)
        grad_acc[...] += dot(grad_pre, up, NT)

    grad_feed = grad_acc[...]
    output[...] = result[...].astype(BF16)
    grad_res = cot_now.astype(F32)
    grad_mid = grad_res + norm_back(grad_feed, gain, normed, inverse)
    grad_mid_out[...] = grad_mid
    branch = grad_mid.astype(BF16)
    grad_mixed_out[...] = dot(branch, w_out[...], NT).astype(BF16)
    acc_out[...] = dot(mixed[...].T, branch).astype(BF16)
    for k, value in enumerate((grad_feed * normed, grad_feed, branch.astype(F32), grad_res)):
        acc_sums[k : k + 1, :] = jnp.sum(value, axis=0, keepdims=True)

    @pl.when(step == pl.num_programs(0) - 1)
    def _():
        for target, steps in zip(targets, leaving):
            for block, far in enumerate(steps):
                spot = slice(block * TILE, (block + 1) * TILE)
                source = me ^ far
                target[spot, :width] = acc_out[rows_at(source), :]
                target[spot, width:edge] = acc_up[rows_at(source), :]
                for fold in range(folds):
                    target[spot, edge + fold * width : edge + (fold + 1) * width] = w_down[
                        rows_at(source * folds + fold), :
                    ]
        sums_out[...] = acc_sums[...]
        sums_up_out[...] = acc_sums_up[...]


def feed(me, tokens, mixed, cotangent, sources, apart, leaving, vec, b_up):
    rows, width = tokens.shape
    block = rows
    columns = sources[0].shape[1]
    hidden = (columns - width) // 2
    blocked = pl.BlockSpec((block, width), lambda i: (i, 0))
    return call(
        functools.partial(feed_kernel, apart, leaving),
        (rows // block,),
        [
            pl.BlockSpec(memory_space=pltpu.SMEM),
            blocked,
            blocked,
            blocked,
            whole(vec.shape),
            whole(b_up.shape),
        ]
        + [pl.BlockSpec(memory_space=pltpu.VMEM) for _ in sources],
        [
            blocked,
            blocked,
            blocked,
        ]
        + [pl.BlockSpec(memory_space=pltpu.VMEM) for _ in leaving]
        + [
            whole((8, width)),
            whole(b_up.shape),
        ],
        [
            jax.ShapeDtypeStruct((rows, width), BF16),
            jax.ShapeDtypeStruct((rows, width), F32),
            jax.ShapeDtypeStruct((rows, width), BF16),
        ]
        + [jax.ShapeDtypeStruct((len(steps) * TILE, columns), BF16) for steps in leaving]
        + [
            jax.ShapeDtypeStruct((8, width), F32),
            jax.ShapeDtypeStruct(b_up.shape, F32),
        ],
        12 * rows * width * hidden + 6 * rows * width * width,
        scratch=[
            pltpu.VMEM((width, width), BF16),
            pltpu.VMEM((width, hidden), BF16),
            pltpu.VMEM((hidden, width), BF16),
            pltpu.VMEM((width, hidden), BF16),
            pltpu.VMEM((width, width), BF16),
            pltpu.VMEM((8, width), F32),
            pltpu.VMEM(b_up.shape, F32),
            pltpu.VMEM((rows, width), F32),
            pltpu.VMEM((rows, width), F32),
        ],
        exps=2 * rows * hidden,
        name="feed",
        vmem=46,
    )(me, tokens, mixed, cotangent, vec, b_up, *sources)


def finish_kernel(own, tok, vec, grad_mid, w, feed_sums, up_sums, proj_sums, grad_proj, grad_out, sums_out, acc):
    step = pl.program_id(0)
    normed, inverse = normalize(tok[...].astype(F32) + vec[8:9, :])
    width = tok.shape[1]
    pairs = width // PAIR
    folds = up_sums.shape[1] // LANES
    columns = [w[:, (kind * pairs + k) * PAIR : (kind * pairs + k + 1) * PAIR] for k in range(pairs) for kind in range(3)]
    grad_attn = dot(grad_proj[...], jnp.concatenate(columns, axis=1), NT)
    gain = vec[GAIN_A : GAIN_A + 1, :]
    grad_start = grad_mid[...] + norm_back(grad_attn, gain, normed, inverse)
    grad_out[...] = grad_start

    @pl.when(step == 0)
    def _():
        acc[...] = jnp.zeros_like(acc)

    for k, value in enumerate((grad_start, grad_attn * normed, grad_attn)):
        acc[k : k + 1, :] += jnp.sum(value, axis=0, keepdims=True)

    @pl.when(step == pl.num_programs(0) - 1)
    def _():
        acc[3:7, :] = feed_sums[0:4, :]
        up_high, up_low = split_two(up_sums[...])
        for fold in range(folds):
            place = folded_place(own, folds, fold, (LANES * folds, LANES), 1)
            rows = dot(up_high, place) + dot(up_low, place)
            for k in range(width // LANES):
                acc[7 + fold : 8 + fold, k * LANES : (k + 1) * LANES] = rows[k : k + 1, :]
        for k in range(pairs):
            acc[11:12, k * PAIR : (k + 1) * PAIR] = proj_sums[:, 3 * k * PAIR : (3 * k + 1) * PAIR]
            acc[12:13, k * PAIR : (k + 1) * PAIR] = proj_sums[
                :, (3 * k + 2) * PAIR : (3 * k + 3) * PAIR
            ]
        acc[TIME : TIME + 1, :] = vec[9:10, :]
        high, low = split_two(acc[...].T)
        half = acc.shape[0] // 2
        lane = lax.broadcasted_iota(jnp.int32, (1, acc.shape[0]), 1)
        shifted = pltpu.roll(low.astype(F32), half, 1)
        sums_out[...] = jnp.where(lane < half, high.astype(F32), shifted).astype(BF16)


TIME = 13


def finish(own, tokens, vec, grad_mid, w, feed_sums, up_sums, proj_sums, grad_proj, block=512):
    rows, width = tokens.shape
    blocked = pl.BlockSpec((block, width), lambda i: (i, 0))
    return call(
        functools.partial(finish_kernel, own),
        (rows // block,),
        [
            blocked,
            whole(vec.shape),
            blocked,
            whole(w.shape),
            whole(feed_sums.shape),
            whole(up_sums.shape),
            whole(proj_sums.shape),
            pl.BlockSpec((block, grad_proj.shape[1]), lambda i: (i, 0)),
        ],
        [blocked, whole((width, LANES))],
        [
            jax.ShapeDtypeStruct((rows, width), F32),
            jax.ShapeDtypeStruct((width, LANES), BF16),
        ],
        6 * rows * width * width,
        scratch=[pltpu.VMEM((LANES, width), F32)],
        name="finish",
        vmem=20,
    )(tokens, vec, grad_mid, w, feed_sums, up_sums, proj_sums, grad_proj)


SUM_ROWS = (1, 2, 3, 4, 11, 12, 5, 6)


def collect_kernel(folds, parts, *refs):
    vectors, up, table_out, held = refs[:-3], refs[-3], refs[-2], refs[-1]
    count, own, _ = parts.shape
    lane = lax.broadcasted_iota(jnp.int32, (1, LANES), 1).astype(F32)
    total = jnp.zeros((own, LANES), F32)
    table = jnp.zeros((own, LANES), F32)
    for source in range(count):
        part = parts[source].astype(F32)
        part = part + pltpu.roll(part, LANES // 2, 1)
        total = total + part
        table = table + jnp.where(lane == part[:, TIME : TIME + 1], part[:, 0:1], 0.0)
    held[...] = jnp.zeros_like(held)
    held[0:own, :] = total
    turned = held[...].T
    for k, out in zip(SUM_ROWS, vectors):
        out[...] = turned[k, 0:own]
    wide = turned[7:8, :]
    for fold in range(1, folds):
        wide = wide + pltpu.roll(turned[7 + fold : 8 + fold, :], fold * own, 1)
    up[...] = wide[0, 0 : folds * own]
    table_out[...] = table[:, 0 : table_out.shape[1]]


def collect(parts, steps, folds):
    own = parts.shape[1]
    vmem = pl.BlockSpec(memory_space=pltpu.VMEM)
    return pl.pallas_call(
        functools.partial(collect_kernel, folds),
        in_specs=[vmem],
        out_specs=[vmem] * 10,
        out_shape=[jax.ShapeDtypeStruct((own,), F32)] * 8
        + [jax.ShapeDtypeStruct((own * folds,), F32), jax.ShapeDtypeStruct((own, steps), F32)],
        scratch_shapes=[pltpu.VMEM((LANES, LANES), F32)],
        compiler_params=small(),
        name="collect",
    )(parts)


def settle_kernel(count, *refs):
    parts, outs = refs[:count], refs[count:]
    value = parts[0][...].astype(F32)
    for part in parts[1:]:
        value = value + part[...].astype(F32)
    own = value.shape[0]
    if len(outs) == 1:
        pairs = value.shape[1] // (3 * PAIR)
        for pair in range(pairs):
            for kind in range(3):
                at = (3 * pair + kind) * PAIR
                spot = (kind * pairs + pair) * PAIR
                outs[0][:, spot : spot + PAIR] = value[:, at : at + PAIR]
    else:
        w_out, w_up, w_down = outs
        width = w_out.shape[1]
        edge = width + w_up.shape[1]
        w_out[...] = value[:, :width]
        w_up[...] = value[:, width:edge]
        for fold in range(w_down.shape[0] // own):
            w_down[fold * own : (fold + 1) * own, :] = value[:, edge + fold * width : edge + (fold + 1) * width]


def settle(parts, shapes, name):
    vmem = pl.BlockSpec(memory_space=pltpu.VMEM)
    return pl.pallas_call(
        functools.partial(settle_kernel, len(parts)),
        in_specs=[vmem] * len(parts),
        out_specs=[vmem] * len(shapes),
        out_shape=[jax.ShapeDtypeStruct(shape, F32) for shape in shapes],
        compiler_params=small(),
        name=name,
    )(*parts)


def levels_of(count):
    bits = (count - 1).bit_length()
    if count != 1 << bits:
        raise ValueError("device count")
    return [[0]] + [list(range(at, min(at + 2, bits))) for at in range(1, bits, 2)]


def masks_of(bits):
    return [step << bits[0] for step in range(1 << len(bits))]


def permute(value, mask, count):
    return lax.ppermute(value, "dp", [(device, device ^ mask) for device in range(count)])


def gather_level(value, bits, count):
    return [value] + [permute(value, mask, count) for mask in masks_of(bits)[1:]]


def total(parts):
    result = parts[0].astype(F32)
    for part in parts[1:]:
        result = result + part.astype(F32)
    return result


def reduce_level(pieces, bits, count):
    return [pieces[0]] + [
        permute(piece, mask, count) for piece, mask in zip(pieces[1:], masks_of(bits)[1:])
    ]


def fold_down(rows, folds, own, back):
    width = rows.shape[1] // folds
    old, new = (TILE, own) if back else (own, TILE)
    rows = rows.reshape(-1, old, folds, width).transpose(0, 2, 1, 3)
    rows = rows.reshape(-1, folds, new, width).transpose(0, 2, 1, 3)
    return rows.reshape(-1, folds * width)


def refold(value, folded, folds, own, back):
    if not folded:
        return value
    edge = value.shape[1] - folded
    return jnp.concatenate([value[:, :edge], fold_down(value[:, edge:], folds, own, back)], axis=1)


class Plan:
    def __init__(self, count, own, folds):
        self.count, self.own, self.folds = count, own, folds
        self.levels = levels_of(count)
        self.tiled = own == TILE and len(self.levels) == 3
        index = lax.axis_index("dp").astype(jnp.int32)
        if self.tiled:
            near, middle, far = (masks_of(bits) for bits in self.levels)
            self.apart = tuple(
                tuple(a + b + c for c in far) for a in near for b in middle
            )
            self.leaving = tuple(tuple(a + b + c for b in middle for c in far) for a in near)
            self.me = index.reshape(1)
        else:
            self.index = index
            self.apart = self.leaving = (tuple(range(own * count // TILE)),)
            self.me = jnp.zeros((1,), jnp.int32)

    def spread(self, shard, level):
        return gather_level(shard, self.levels[level], self.count)

    def near(self, halves):
        keep, send = halves
        return keep, permute(send, 1, self.count)

    def cut(self, parts):
        size = parts[0].shape[0] // 4
        return [
            total([part[k * size : (k + 1) * size] for part in parts]).astype(BF16)
            for k in range(4)
        ]

    def around(self, pieces):
        return reduce_level(pieces, self.levels[1], self.count)

    def far(self, pieces):
        return reduce_level(pieces, self.levels[2], self.count)

    def whole(self, shard, folded):
        value = shard
        for bits in reversed(self.levels):
            value = jnp.stack(gather_level(value, bits, self.count))
        value = value.reshape((self.count,) + shard.shape)
        value = value[self.places() ^ self.place(self.index)]
        return refold(value.reshape(-1, shard.shape[1]), folded, self.folds, self.own, False)

    def place(self, device):
        result = 0
        for bits in self.levels:
            result = (result << len(bits)) | ((device >> bits[0]) & ((1 << len(bits)) - 1))
        return result

    def places(self):
        return self.place(jnp.arange(self.count, dtype=jnp.int32))

    def sum_whole(self, value, folded):
        value = refold(value, folded, self.folds, self.own, True)
        value = value.reshape(self.count, self.own, -1)
        order = [0] * self.count
        for device in range(self.count):
            order[self.place(device)] = device
        value = value[jnp.array(order, jnp.int32) ^ self.index]
        for at, bits in enumerate(self.levels):
            value = value.reshape((1 << len(bits), -1) + value.shape[1:])
            value = total(reduce_level(list(value), bits, self.count))
            if at < len(self.levels) - 1:
                value = value.astype(BF16)
        return value.reshape(self.own, -1)


def after(value, *done):
    leaves, tree = jax.tree.flatten(value)
    return jax.tree.unflatten(tree, lax.optimization_barrier((*leaves, *done))[: len(leaves)])


def exchange(value):
    return lax.all_to_all(value, "dp", 0, 0, tiled=True)


def per_device(
    count,
    tokens,
    timesteps,
    w_qkv,
    w_out,
    w_up,
    w_down,
    gain_attn,
    shift_attn,
    gain_ffn,
    shift_ffn,
    bias_query,
    bias_value,
    bias_out,
    bias_up,
    bias_down,
    step_table,
    cotangent,
):
    rows, width = tokens.shape
    own = width // count
    steps = step_table.shape[0]
    hidden = w_up.shape[1]
    folds = hidden // width
    edge = width + hidden
    plan = Plan(count, own, folds)
    pairs = width // PAIR

    vectors = (
        gain_attn,
        shift_attn,
        gain_ffn,
        shift_ffn,
        bias_query,
        bias_value,
        bias_out,
        bias_down,
    )
    plan.me = after(plan.me, w_qkv)
    w_qkv = after(w_qkv, plan.me)
    entry = pack(w_qkv, step_table, vectors, bias_up)
    if plan.tiled:
        joint = join(w_out, w_up, w_down)
        far = plan.spread(entry, 2)
        joint = plan.spread(joint, 2)
        entry = jnp.concatenate(far, axis=0)
        entries = plan.spread(entry, 1)
        joint = jnp.concatenate(after(joint, *entries[1:]), axis=0)
        entries = entries + [permute(entry, 1, count) for entry in entries]
        joints = plan.spread(joint, 1)
    else:
        joint = jnp.concatenate(
            [w_out, w_up] + [w_down[k * own : (k + 1) * own] for k in range(folds)], axis=1
        )
        entries = [plan.whole(entry, 0)]
        joints = [plan.whole(joint, hidden)]

    proj, turned, full_qkv, vec, up_bias = project(
        plan.me, timesteps, tokens, entries, plan.apart, own, folds
    )
    mixed, stats = attend(proj)

    if plan.tiled:
        joints[1:] = after(joints[1:], mixed)
        joints = joints + [permute(joint, 1, count) for joint in joints]
    feed_out = feed(
        plan.me, tokens, mixed, cotangent, joints, plan.apart, plan.leaving, vec, up_bias
    )
    output, grad_mid, grad_mixed = feed_out[:3]
    feed_sums, up_sums = feed_out[-2:]

    def back(grad_mixed, begin, number, before=()):
        return attend_back(
            plan.me, plan.leaving, proj, grad_mixed, mixed, stats, turned, begin, number, before
        )

    if plan.tiled:
        near = plan.near(feed_out[3:5])
        first = back(grad_mixed, 0, 1)
        pieces = plan.cut(after(near, first[0]))
        grad_proj, proj_sums, *leaving = back(after(grad_mixed, *pieces), 1, pairs - 1, first)
        pieces = plan.cut(after(plan.around(pieces), grad_proj))
        near = plan.near(after(leaving, *pieces))
        leaving = plan.cut(near)
        grad_mid = after(grad_mid, *leaving)
    else:
        grad_proj, proj_sums, leaving = back(grad_mixed, 0, pairs)
        sum_parts = [plan.sum_whole(feed_out[3], hidden)]
        weight_parts = [plan.sum_whole(leaving, 0)]

    grad_start, packed_sums = finish(
        own, tokens, vec, grad_mid, full_qkv, feed_sums, up_sums, proj_sums, grad_proj
    )
    parts = exchange(packed_sums.reshape(count, own, LANES))
    if plan.tiled:
        sum_parts = plan.far(pieces)
        pieces = after(plan.around(leaving), grad_start)
        weight_parts = plan.far(plan.cut(pieces))
    *sums, sum_up, sum_table = collect(parts, steps, folds)
    sum_out, sum_w_up, sum_down = settle(
        sum_parts, (w_out.shape, w_up.shape, w_down.shape), "settle_joint"
    )
    (sum_qkv,) = settle(weight_parts, (w_qkv.shape,), "settle_qkv")
    return (
        output,
        grad_start,
        sum_qkv,
        sum_out,
        sum_w_up,
        sum_down,
        *sums[:7],
        sum_up,
        sums[7],
        sum_table.T,
    )


def solution(mesh):
    in_specs = (
        P("dp", None),
        P("dp"),
        P("dp", None),
        P("dp", None),
        P("dp", None),
        P("dp", None),
        P("dp"),
        P("dp"),
        P("dp"),
        P("dp"),
        P("dp"),
        P("dp"),
        P("dp"),
        P("dp"),
        P("dp"),
        P(None, "dp"),
        P("dp", None),
    )
    out_specs = (
        P("dp", None),
        P("dp", None),
        P("dp", None),
        P("dp", None),
        P("dp", None),
        P("dp", None),
        P("dp"),
        P("dp"),
        P("dp"),
        P("dp"),
        P("dp"),
        P("dp"),
        P("dp"),
        P("dp"),
        P("dp"),
        P(None, "dp"),
    )
    return jax.shard_map(
        functools.partial(per_device, mesh.shape["dp"]), mesh=mesh, in_specs=in_specs, out_specs=out_specs, check_vma=False
    )
```
